512 devices in a mesh: dp: 64 (over x, y, core), tensor: 4 (over z_hi), replica: 2 (over z_lo).
Axes of the slice: x: 4, y: 8, z: 8 (z_hi: 4, z_lo: 2; z = z_hi * 2 + z_lo), core: 2. Of those that a mesh axis runs over, the one named last changes fastest.
Arguments:
- features: bfloat16 [128, 1536, 1024], P(('dp', 'replica'), 'tensor'), may hold values from -600 to 600
- cotangents: bfloat16 [128, 1536, 2, 1024], P(('dp', 'replica'), None, None, 'tensor'), may hold values from -150 to 150
- moment_one: float32 [2, 1024, 1024], P(None, ('dp', 'replica'), 'tensor'), may hold values from -6 to 6
- moment_two: float32 [2, 1024, 1024], P(None, ('dp', 'replica'), 'tensor'), may hold values from 0.01 to 4
- master: float32 [2, 1024, 1024], P(None, ('dp', 'replica'), 'tensor'), may hold values from -6 to 6
- average: float32 [128, 4, 4, 1024], P(('dp', 'replica'), 'tensor'), may hold values from -6 to 6
Outputs:
- weights: bfloat16 [2, 1024, 1024], P(None, None, 'tensor')
- new_first: float32 [2, 1024, 1024], P(None, ('dp', 'replica'), 'tensor')
- new_second: float32 [2, 1024, 1024], P(None, ('dp', 'replica'), 'tensor')
- new_master: float32 [2, 1024, 1024], P(None, ('dp', 'replica'), 'tensor')
- new_average: float32 [128, 4, 4, 1024], P(('dp', 'replica'), 'tensor')
The draws below stay inside these ranges and needn't reach their ends.
All inputs are finite; a program needn't handle non-finite values.
Results may differ from the reference program's by a relative error of at most 0.0055.
Values may be sent and summed in bfloat16 or wider, within the bound.
No kernel may reach another device: no remote copies, remote signals or barrier semaphores. Data moves between devices by JAX's collectives and lax.ppermute only.
A program may use at most 64 MiB of HBM per device.

```python
import math
import jax
import jax.numpy as jnp
from jax import lax

D = 1024
TOK_DEV = 1536
STEP = 100
GROUPS = 128
ROW_PIECE = 8
AVG_ROWS = 4
N_TENSOR = 4


def draw_features(key, part):
    shape = (GROUPS, TOK_DEV, D)
    key_noise = jax.random.fold_in(key, 11)
    key_spread = jax.random.fold_in(key, 13)
    key_order = jax.random.fold_in(key, 14)
    position = jnp.arange(D, dtype=jnp.float32) / D
    spread = jnp.exp(jax.random.uniform(key_spread, (D,), jnp.float32) * jnp.log(10.0))
    noise = jnp.clip(jax.random.normal(key_noise, shape, jnp.float32), -4.0, 4.0)
    trend = 3.0 ** (0.5 * position)
    order = jax.random.permutation(key_order, GROUPS)
    block_index = jnp.arange(D) // (D // GROUPS)
    boost = jnp.where(block_index[None, :] == order[:, None], 4.0, 1.0)
    values = noise * (spread * trend)[None, None, :] * boost[:, None, :]
    return values.astype(jnp.bfloat16)


def draw_cotangents(key, part):
    shape = (GROUPS, TOK_DEV, 2, D)
    key_noise = jax.random.fold_in(key, 21)
    key_spread = jax.random.fold_in(key, 23)
    position = jnp.arange(D, dtype=jnp.float32) / D
    spread = jnp.exp(jax.random.uniform(key_spread, (2, D), jnp.float32) * jnp.log(10.0))
    noise = jnp.clip(jax.random.normal(key_noise, shape, jnp.float32), -4.0, 4.0)
    trend = 3.0 ** (0.5 * position)
    values = noise * (spread * trend[None, :])[None, None, :, :]
    return values.astype(jnp.bfloat16)


def block_scale(rng, shape, split, smallest, high):
    def one(axis_at, shards_of):
        steps = jax.random.uniform(jax.random.fold_in(jax.random.fold_in(rng, 6), axis_at), (shards_of,), jnp.float32, smallest / len(split), high / len(split))
        return jnp.repeat(jnp.exp(steps), shape[axis_at] // shards_of).reshape((-1,) + (1,) * (len(shape) - axis_at - 1))

    level = one(*split[0])
    for cut in split[1:]:
        level = level * one(*cut)
    return level


def gaussian(rng, dims, deviation, reach, shards=(), held_as=jnp.bfloat16):
    level = block_scale(rng, dims, shards, -0.22, 0.18) if shards else 1.0
    entries = jax.random.normal(rng, dims, jnp.float32) * deviation * level
    return jnp.minimum(jnp.maximum(entries, -reach), reach).astype(held_as)


def setup_inputs(seed: int = 0) -> dict:
    seeds = jax.random.split(jax.random.key(seed), 7)
    features = draw_features(jax.random.fold_in(seeds[6], 71), 0)
    cotangents = draw_cotangents(jax.random.fold_in(seeds[6], 71), 0)
    moment_one = gaussian(seeds[2], (2, D, D), 1.0, 6.0, ((1, 128), (2, 4)), jnp.float32)
    moment_two = jnp.clip(jnp.exp(math.log(4.0) - 5.9914646 * jax.random.uniform(seeds[3], (2, D, D), jnp.float32) ** block_scale(seeds[3], (2, D, D), ((1, 128), (2, 4)), -0.2, 0.2)), 0.01, 4.0)
    master = gaussian(seeds[4], (2, D, D), 1.0, 6.0, ((1, 128), (2, 4)), jnp.float32)
    average = gaussian(seeds[5], (GROUPS, N_TENSOR, AVG_ROWS, D), 1.0, 6.0, ((0, 128), (1, 4)), jnp.float32)
    return {"features": features, "cotangents": cotangents, "moment_one": moment_one, "moment_two": moment_two, "master": master, "average": average}


beta_one = 0.9
beta_two = 0.95
learn_rate = 0.05
decay_rate = 0.1
adam_eps = 1e-08
average_keep = 0.9

def reference(features, cotangents, moment_one, moment_two, master, average):
    token_rows = features.reshape(GROUPS * TOK_DEV, D)
    output_rows = cotangents.reshape(GROUPS * TOK_DEV, 2 * D)
    gradient = lax.dot_general(token_rows, output_rows, (((0,), (0,)), ((), ())), preferred_element_type=jnp.float32)
    gradient = jnp.transpose(gradient.reshape(D, 2, D), (1, 0, 2))
    square_total = jnp.sum(gradient * gradient)
    clip_factor = 1.0 / jnp.sqrt(square_total / (2.0 * D * D) + 1e-06)
    scaled = clip_factor * gradient
    new_first = beta_one * moment_one + (1.0 - beta_one) * scaled
    new_second = beta_two * moment_two + (1.0 - beta_two) * (scaled * scaled)
    fix_one = 1.0 - beta_one ** STEP
    fix_two = 1.0 - beta_two ** STEP
    direction = new_first / fix_one / (jnp.sqrt(new_second / fix_two) + adam_eps)
    new_master = master - learn_rate * (direction + decay_rate * master)
    weights = new_master.astype(jnp.bfloat16)
    blocks = new_master.reshape(2, GROUPS, ROW_PIECE, D)
    blocks = jnp.transpose(blocks, (1, 0, 2, 3)).reshape(GROUPS, N_TENSOR, AVG_ROWS, D)
    new_average = average_keep * average + (1.0 - average_keep) * blocks
    return (weights, new_first, new_second, new_master, new_average)
```

```python
import jax
import jax.numpy as jnp
from jax import lax
from jax.sharding import Mesh, PartitionSpec as P

STEP = 100


beta_one = 0.9
beta_two = 0.95
learn_rate = 0.05
decay_rate = 0.1
adam_eps = 1e-08
average_keep = 0.9

XYR = ("x", "y", "replica")
SWAP = ((0, 1), (1, 0))


def shards(features, cotangents, moment_one, moment_two, master, average):
    f32, bf16 = jnp.float32, jnp.bfloat16
    col_width = cotangents.shape[3]
    rows = moment_one.shape[1]
    nx, ny, nr = (lax.axis_size(name) for name in XYR)
    peers = nx * ny * nr
    core = lax.axis_index("core")

    tokens_all = lax.all_gather(features, "tensor", axis=1, tiled=True)[0]
    dim_model = tokens_all.shape[1]
    outgrad = cotangents[0].reshape(cotangents.shape[1], 2 * col_width)
    product = lax.dot_general(
        tokens_all, outgrad, (((0,), (0,)), ((), ())), preferred_element_type=f32
    )
    pieces = product.reshape(nx * ny, 2, nr, rows, 2 * col_width)
    keep = lax.dynamic_index_in_dim(pieces, core, axis=1, keepdims=False)
    give = lax.dynamic_index_in_dim(pieces, 1 - core, axis=1, keepdims=False)
    got = lax.ppermute(give.astype(bf16), "core", SWAP)
    half = (keep + got.astype(f32)).astype(bf16).reshape(peers, rows, 2 * col_width)
    terms = lax.all_to_all(half, XYR, split_axis=0, concat_axis=0, tiled=True)
    grad_piece = jnp.sum(terms.astype(f32), axis=0).reshape(rows, 2, col_width)
    gradient = jnp.transpose(grad_piece, (1, 0, 2))

    square_total = jnp.sum(gradient * gradient)
    for names in ("core", "x", "y", ("tensor", "replica")):
        square_total = lax.psum(square_total, names)
    count_all = 2.0 * dim_model * dim_model
    clip_factor = 1.0 / jnp.sqrt(square_total / count_all + 1e-06)
    scaled = clip_factor * gradient
    new_first = beta_one * moment_one + (1.0 - beta_one) * scaled
    new_second = beta_two * moment_two + (1.0 - beta_two) * (scaled * scaled)
    fix_one = 1.0 - beta_one**STEP
    fix_two = 1.0 - beta_two**STEP
    direction = new_first / fix_one / (jnp.sqrt(new_second / fix_two) + adam_eps)
    new_master = master - learn_rate * (direction + decay_rate * master)

    mine = new_master.astype(bf16)
    spread = jnp.broadcast_to(mine[None], (peers,) + mine.shape)
    column = lax.all_to_all(spread, XYR, split_axis=0, concat_axis=0, tiled=True)
    other = lax.ppermute(column, "core", SWAP)
    even = jnp.where(core == 0, column, other)
    odd = jnp.where(core == 0, other, column)
    both = jnp.stack([even, odd]).reshape(2, nx * ny, nr, 2, rows, col_width)
    weights = jnp.transpose(both, (3, 1, 0, 2, 4, 5)).reshape(2, dim_model, col_width)

    flat_rows = new_master.reshape(2 * rows, col_width)
    row_flat = lax.all_to_all(flat_rows, "tensor", split_axis=0, concat_axis=1, tiled=True)
    new_average = average_keep * average + (1.0 - average_keep) * row_flat.reshape(average.shape)
    return (weights, new_first, new_second, new_master, new_average)


def solution(mesh):
    shape = dict(zip(mesh.axis_names, mesh.devices.shape))
    nx, ny = 4, shape["dp"] // 8
    fine = Mesh(
        mesh.devices.reshape(nx, ny, 2, shape["tensor"], shape["replica"]),
        ("x", "y", "core", "tensor", "replica"),
    )
    groups = ("x", "y", "core", "replica")
    state = P(None, groups, "tensor")
    placed = (
        P(groups, "tensor", None),
        P(groups, None, None, "tensor"),
        state,
        state,
        state,
        P(groups, "tensor", None, None),
    )
    return jax.shard_map(
        shards,
        mesh=fine,
        in_specs=placed,
        out_specs=(P(None, None, "tensor"), state, state, state, P(groups, "tensor", None, None)),
        check_vma=False,
    )
```

```python
import jax
import jax.numpy as jnp
from jax import lax
from jax.experimental import pallas as pl
from jax.experimental.pallas import tpu as pltpu
from jax.sharding import Mesh, PartitionSpec as P

STEP = 100


beta_one = 0.9
beta_two = 0.95
learn_rate = 0.05
decay_rate = 0.1
adam_eps = 1e-08
average_keep = 0.9

XYR = ("x", "y", "replica")
SWAP = ((0, 1), (1, 0))


def round_trip(count, step):
    return [(i, (i + step) % count) for i in range(count)]


def along_tokens(block, against):
    return lax.dot_general(
        block, against, (((0,), (0,)), ((), ())), preferred_element_type=jnp.float32
    )


def near_kernel(where, own, low_first, high_second, low_second, high_first, outgrad, _, total):
    count, part = own.shape[0], low_first.shape[0]
    shards_all = outgrad.shape[0] // count

    def against(step, half, size):
        start = lax.rem(where[0] + step, shards_all) * count + half * part
        return outgrad[pl.ds(pl.multiple_of(start, part), size), :]

    total[...] = (
        along_tokens(own[...], against(0, 0, count))
        + along_tokens(low_first[...], against(shards_all - 1, 0, part))
        + along_tokens(low_second[...], against(shards_all - 1, 1, part))
        + along_tokens(high_first[...], against(1, 0, part))
        + along_tokens(high_second[...], against(1, 1, part))
    )


def far_kernel(where, total, far_first, far_second, outgrad, keep, give):
    part = far_first.shape[0]
    start = lax.rem(where[0] + 2, outgrad.shape[0] // (2 * part)) * (2 * part)
    against = outgrad[pl.ds(pl.multiple_of(start, part), 2 * part), :]
    value = (
        total[...]
        + along_tokens(far_first[...], against[:part])
        + along_tokens(far_second[...], against[part:])
    )
    lines, width = keep.shape[1], keep.shape[2]
    value = value.reshape(keep.shape[0], 2, lines, width)
    even, odd = value[:, 0], value[:, 1]
    first_core = where[1] == 0
    keep[...] = jnp.where(first_core, even, odd)
    give[...] = jnp.where(first_core, odd, even).astype(give.dtype)


def shards(features, cotangents, moment_one, moment_two, master, average):
    f32, bf16 = jnp.float32, jnp.bfloat16
    col_width = cotangents.shape[3]
    rows = moment_one.shape[1]
    nx, ny, nr = (lax.axis_size(name) for name in XYR)
    nt = lax.axis_size("tensor")
    peers = nx * ny * nr
    core = lax.axis_index("core")
    place = lax.axis_index("tensor")
    where = jnp.stack([place, core]).astype(jnp.int32)

    tokens = features[0]
    count, dim_model = tokens.shape
    part = count // 2
    first, second = tokens[:part], tokens[part:]
    up, down = round_trip(nt, 1), round_trip(nt, nt - 1)
    low_first = lax.ppermute(first, "tensor", up)
    high_second = lax.ppermute(second, "tensor", down)
    low_second = lax.ppermute(second, "tensor", up)
    high_first = lax.ppermute(first, "tensor", down)
    far_first = lax.ppermute(low_first, "tensor", up)
    far_second = lax.ppermute(high_second, "tensor", down)
    outgrad = cotangents[0].reshape(cotangents.shape[1], 2 * col_width)

    held_rows = 2 * rows // nt
    state = jnp.stack([moment_one, moment_two, master])
    state = state.reshape(3, nt, held_rows, col_width).transpose(1, 0, 2, 3)
    state = lax.all_to_all(state, "tensor", 0, 0, tiled=True)

    tile = dim_model // nx
    width = 2 * col_width
    lines = nr * rows
    whole = pl.BlockSpec(outgrad.shape, lambda i, w: (0, 0))
    piece = pl.BlockSpec((part, tile), lambda i, w: (0, i))
    block = pl.BlockSpec((tile, width), lambda i, w: (i, 0))
    split = pl.BlockSpec((ny, lines, width), lambda i, w: (i, 0, 0))
    total = pl.pallas_call(
        near_kernel,
        out_shape=jax.ShapeDtypeStruct((dim_model, width), f32),
        grid_spec=pltpu.PrefetchScalarGridSpec(
            num_scalar_prefetch=1,
            grid=(nx,),
            in_specs=[
                pl.BlockSpec((count, tile), lambda i, w: (0, i)),
                piece,
                piece,
                piece,
                piece,
                whole,
                pl.BlockSpec(memory_space=pl.ANY),
            ],
            out_specs=block,
        ),
        cost_estimate=pl.CostEstimate(
            flops=6 * count * dim_model * width, bytes_accessed=8 * 2**20, transcendentals=0
        ),
    )(where, tokens, low_first, high_second, low_second, high_first, outgrad, state)
    keep, give = pl.pallas_call(
        far_kernel,
        out_shape=(
            jax.ShapeDtypeStruct((nx * ny, lines, width), f32),
            jax.ShapeDtypeStruct((nx * ny, lines, width), bf16),
        ),
        grid_spec=pltpu.PrefetchScalarGridSpec(
            num_scalar_prefetch=1,
            grid=(nx,),
            in_specs=[block, piece, piece, whole],
            out_specs=(split, split),
        ),
        cost_estimate=pl.CostEstimate(
            flops=2 * count * dim_model * width, bytes_accessed=6 * 2**20, transcendentals=0
        ),
    )(where, total, far_first, far_second, outgrad)

    got = lax.ppermute(give, "core", SWAP)
    half = (keep + got.astype(f32)).astype(bf16).reshape(peers, rows, width)
    terms = lax.all_to_all(half, XYR, split_axis=0, concat_axis=0, tiled=True)
    grad_piece = jnp.sum(terms.astype(f32), axis=0).reshape(rows, 2, col_width)
    gradient = jnp.transpose(grad_piece, (1, 0, 2))

    flat = gradient.reshape(nt, held_rows, col_width)
    squares = jnp.sum(flat * flat, axis=(0, 1))
    mixed = jnp.concatenate([flat, jnp.broadcast_to(squares, flat.shape)], axis=1)
    mixed = lax.all_to_all(mixed, "tensor", 0, 0, tiled=True)
    row_grad = mixed[:, :held_rows]
    squares = jnp.sum(mixed[:, held_rows], axis=0)
    others = ("x", "y", "core", "replica")
    spread = jnp.broadcast_to(squares, (lax.axis_size(others), col_width))
    squares = jnp.sum(lax.all_to_all(spread, others, 0, 0, tiled=True))
    count_all = 2.0 * dim_model * dim_model
    clip_factor = 1.0 / jnp.sqrt(squares / count_all + 1e-06)

    fix_one = 1.0 - beta_one**STEP
    fix_two = 1.0 - beta_two**STEP

    def update(grad, one, two, held):
        scaled = clip_factor * grad
        new_one = beta_one * one + (1.0 - beta_one) * scaled
        new_two = beta_two * two + (1.0 - beta_two) * (scaled * scaled)
        direction = new_one / fix_one / (jnp.sqrt(new_two / fix_two) + adam_eps)
        return new_one, new_two, held - learn_rate * (direction + decay_rate * held)

    new_first, new_second, new_master = update(gradient, moment_one, moment_two, master)

    mine = new_master.astype(bf16)
    spread = jnp.broadcast_to(mine[None], (peers,) + mine.shape)
    column = lax.all_to_all(spread, XYR, split_axis=0, concat_axis=0, tiled=True)
    other = lax.ppermute(column, "core", SWAP)
    even = jnp.where(core == 0, column, other)
    odd = jnp.where(core == 0, other, column)
    both = jnp.stack([even, odd]).reshape(2, nx * ny, nr, 2, rows, col_width)
    weights = jnp.transpose(both, (3, 1, 0, 2, 4, 5)).reshape(2, dim_model, col_width)

    row_master = update(row_grad, state[:, 0], state[:, 1], state[:, 2])[2]
    row_master = jnp.transpose(row_master, (1, 0, 2)).reshape(average.shape)
    new_average = average_keep * average + (1.0 - average_keep) * row_master
    return (weights, new_first, new_second, new_master, new_average)


def solution(mesh):
    shape = dict(zip(mesh.axis_names, mesh.devices.shape))
    nx, ny = 4, shape["dp"] // 8
    fine = Mesh(
        mesh.devices.reshape(nx, ny, 2, shape["tensor"], shape["replica"]),
        ("x", "y", "core", "tensor", "replica"),
    )
    groups = ("x", "y", "core", "replica")
    state = P(None, groups, "tensor")
    placed = (
        P(groups, "tensor", None),
        P(groups, None, None, "tensor"),
        state,
        state,
        state,
        P(groups, "tensor", None, None),
    )
    return jax.shard_map(
        shards,
        mesh=fine,
        in_specs=placed,
        out_specs=(P(None, None, "tensor"), state, state, state, P(groups, "tensor", None, None)),
        check_vma=False,
    )
```

```python
import jax
import jax.numpy as jnp
from jax import lax
from jax.experimental import pallas as pl
from jax.experimental.pallas import tpu as pltpu
from jax.sharding import Mesh, PartitionSpec as P

STEP = 100


beta_one = 0.9
beta_two = 0.95
learn_rate = 0.05
decay_rate = 0.1
adam_eps = 1e-08
average_keep = 0.9

XYR = ("x", "y", "replica")
SWAP = ((0, 1), (1, 0))


def round_trip(count, step):
    return [(i, (i + step) % count) for i in range(count)]


def along_tokens(block, against):
    return lax.dot_general(
        block, against, (((0,), (0,)), ((), ())), preferred_element_type=jnp.float32
    )


def near_kernel(where, own, low, high, outgrad, total):
    count = own.shape[0]
    shards_all = outgrad.shape[0] // count
    tile = 256

    def against(step):
        start = lax.rem(where[0] + step, shards_all) * count
        return outgrad[pl.ds(pl.multiple_of(start, count), count), :]

    for left in range(0, own.shape[1], tile):
        part = slice(left, left + tile)
        total[part, :] = (
            along_tokens(own[:, part], against(0))
            + along_tokens(low[:, part], against(shards_all - 1))
            + along_tokens(high[:, part], against(1))
        )


def far_kernel(where, total, far_first, far_second, outgrad, keep, give):
    part = far_first.shape[0]
    start = lax.rem(where[0] + 2, outgrad.shape[0] // (2 * part)) * (2 * part)
    against = outgrad[pl.ds(pl.multiple_of(start, 2 * part), 2 * part), :]
    first_core = where[1] == 0
    lines, width = keep.shape[1], keep.shape[2]
    tile = 256
    for left in range(0, total.shape[0], tile):
        cut = slice(left, left + tile)
        value = (
            total[cut, :]
            + along_tokens(far_first[:, cut], against[:part])
            + along_tokens(far_second[:, cut], against[part:])
        )
        value = value.reshape(tile // (2 * lines), 2, lines, width)
        even, odd = value[:, 0], value[:, 1]
        out = slice(left // (2 * lines), (left + tile) // (2 * lines))
        keep[out] = jnp.where(first_core, even, odd)
        give[out] = jnp.where(first_core, odd, even).astype(give.dtype)


def shards(features, cotangents, moment_one, moment_two, master, average):
    f32, bf16 = jnp.float32, jnp.bfloat16
    col_width = cotangents.shape[3]
    rows = moment_one.shape[1]
    nx, ny, nr = (lax.axis_size(name) for name in XYR)
    nt = lax.axis_size("tensor")
    peers = nx * ny * nr
    core = lax.axis_index("core")
    place = lax.axis_index("tensor")
    where = jnp.stack([place, core]).astype(jnp.int32)

    tokens = features[0]
    count, dim_model = tokens.shape
    part = count // 2
    up, down = round_trip(nt, 1), round_trip(nt, nt - 1)
    low = lax.ppermute(tokens, "tensor", up)
    high = lax.ppermute(tokens, "tensor", down)
    far_first = lax.ppermute(low[:part], "tensor", up)
    far_second = lax.ppermute(high[part:], "tensor", down)
    outgrad = cotangents[0].reshape(cotangents.shape[1], 2 * col_width)

    width = 2 * col_width
    lines = nr * rows
    scalars = pl.BlockSpec(memory_space=pltpu.SMEM)
    local = pl.BlockSpec(memory_space=pltpu.VMEM)
    params = pltpu.CompilerParams(vmem_limit_bytes=24 * 2**20)
    total = pl.pallas_call(
        near_kernel,
        out_shape=jax.ShapeDtypeStruct((dim_model, width), f32),
        in_specs=[scalars] + [local] * 4,
        out_specs=local,
        compiler_params=params,
        cost_estimate=pl.CostEstimate(
            flops=6 * count * dim_model * width, bytes_accessed=6 * 2**20, transcendentals=0
        ),
    )(where, tokens, low, high, outgrad)
    keep, give = pl.pallas_call(
        far_kernel,
        out_shape=(
            jax.ShapeDtypeStruct((nx * ny, lines, width), f32),
            jax.ShapeDtypeStruct((nx * ny, lines, width), bf16),
        ),
        in_specs=[scalars] + [local] * 4,
        out_specs=(local, local),
        compiler_params=params,
        cost_estimate=pl.CostEstimate(
            flops=2 * count * dim_model * width, bytes_accessed=6 * 2**20, transcendentals=0
        ),
    )(where, total, far_first, far_second, outgrad)

    got = lax.ppermute(give, "core", SWAP)
    half = (keep + got.astype(f32)).astype(bf16).reshape(peers, rows, width)
    terms = lax.all_to_all(half, XYR, split_axis=0, concat_axis=0, tiled=True)
    grad_piece = jnp.sum(terms.astype(f32), axis=0).reshape(rows, 2, col_width)
    gradient = jnp.transpose(grad_piece, (1, 0, 2))

    held_rows = 2 * rows // nt
    by_rows = lambda block: block.reshape(nt, held_rows, col_width)
    flat = by_rows(gradient)
    squares = jnp.broadcast_to(jnp.sum(flat * flat, axis=(0, 1)), flat.shape)
    mixed = [flat, by_rows(moment_one), by_rows(moment_two), by_rows(master), squares]
    mixed = lax.all_to_all(jnp.concatenate(mixed, axis=1), "tensor", 0, 0, tiled=True)
    row_grad, row_one, row_two, row_held, squares = jnp.split(mixed, 5, axis=1)
    squares = jnp.sum(squares[:, 0], axis=0)
    others = ("x", "y", "core", "replica")
    spread = jnp.broadcast_to(squares, (lax.axis_size(others), col_width))
    squares = jnp.sum(lax.all_to_all(spread, others, 0, 0, tiled=True))
    count_all = 2.0 * dim_model * dim_model
    clip_factor = 1.0 / jnp.sqrt(squares / count_all + 1e-06)

    fix_one = 1.0 - beta_one**STEP
    fix_two = 1.0 - beta_two**STEP

    def update(grad, one, two, held):
        scaled = clip_factor * grad
        new_one = beta_one * one + (1.0 - beta_one) * scaled
        new_two = beta_two * two + (1.0 - beta_two) * (scaled * scaled)
        direction = new_one / fix_one / (jnp.sqrt(new_two / fix_two) + adam_eps)
        return new_one, new_two, held - learn_rate * (direction + decay_rate * held)

    new_first, new_second, new_master = update(gradient, moment_one, moment_two, master)

    mine = new_master.astype(bf16)
    spread = jnp.broadcast_to(mine[None], (peers,) + mine.shape)
    column = lax.all_to_all(spread, XYR, split_axis=0, concat_axis=0, tiled=True)
    other = lax.ppermute(column, "core", SWAP)
    even = jnp.where(core == 0, column, other)
    odd = jnp.where(core == 0, other, column)
    both = jnp.stack([even, odd]).reshape(2, nx * ny, nr, 2, rows, col_width)
    weights = jnp.transpose(both, (3, 1, 0, 2, 4, 5)).reshape(2, dim_model, col_width)

    row_master = update(row_grad, row_one, row_two, row_held)[2]
    row_master = jnp.transpose(row_master, (1, 0, 2)).reshape(average.shape)
    new_average = average_keep * average + (1.0 - average_keep) * row_master
    return (weights, new_first, new_second, new_master, new_average)


def solution(mesh):
    shape = dict(zip(mesh.axis_names, mesh.devices.shape))
    nx, ny = 4, shape["dp"] // 8
    fine = Mesh(
        mesh.devices.reshape(nx, ny, 2, shape["tensor"], shape["replica"]),
        ("x", "y", "core", "tensor", "replica"),
    )
    groups = ("x", "y", "core", "replica")
    state = P(None, groups, "tensor")
    placed = (
        P(groups, "tensor", None),
        P(groups, None, None, "tensor"),
        state,
        state,
        state,
        P(groups, "tensor", None, None),
    )
    return jax.shard_map(
        shards,
        mesh=fine,
        in_specs=placed,
        out_specs=(P(None, None, "tensor"), state, state, state, P(groups, "tensor", None, None)),
        check_vma=False,
    )
```

```python
import jax
import jax.numpy as jnp
from jax import lax
from jax.experimental import pallas as pl
from jax.experimental.pallas import tpu as pltpu
from jax.sharding import Mesh, PartitionSpec as P

STEP = 100


beta_one = 0.9
beta_two = 0.95
learn_rate = 0.05
decay_rate = 0.1
adam_eps = 1e-08
average_keep = 0.9

XYR = ("x", "y", "replica")
PLANE = ("x", "y")
SWAP = ((0, 1), (1, 0))


def gather_plane(block):
    peers = lax.axis_size(PLANE)
    spread = jnp.broadcast_to(block[None], (peers,) + block.shape)
    return lax.all_to_all(spread, PLANE, 0, 0, tiled=True)


def round_trip(count, step):
    return [(i, (i + step) % count) for i in range(count)]


def along_tokens(block, against):
    return lax.dot_general(
        block, against, (((0,), (0,)), ((), ())), preferred_element_type=jnp.float32
    )


def state_kernel(one, two, held, wide):
    bf16 = jnp.bfloat16
    peers, _, _, width = wide.shape
    col_width = width // 2
    for half in range(2):
        master = held[half]
        high = master.astype(bf16)
        low = (master - high.astype(jnp.float32)).astype(bf16)
        for k, block in enumerate((one[half].astype(bf16), two[half].astype(bf16), high, low)):
            columns = slice(half * col_width, (half + 1) * col_width)
            wide[:, k, :, columns] = jnp.broadcast_to(block[None], (peers,) + block.shape)


def near_kernel(where, own, low, high, outgrad, total):
    count = own.shape[0]
    shards_all = outgrad.shape[0] // count
    tile = 256

    def against(step):
        start = lax.rem(where[0] + step, shards_all) * count
        return outgrad[pl.ds(pl.multiple_of(start, count), count), :]

    for left in range(0, own.shape[1], tile):
        part = slice(left, left + tile)
        total[part, :] = (
            along_tokens(own[:, part], against(0))
            + along_tokens(low[:, part], against(shards_all - 1))
            + along_tokens(high[:, part], against(1))
        )


def far_kernel(where, total, far_first, far_second, outgrad, _, keep, give):
    part = far_first.shape[0]
    start = lax.rem(where[0] + 2, outgrad.shape[0] // (2 * part)) * (2 * part)
    against = outgrad[pl.ds(pl.multiple_of(start, 2 * part), 2 * part), :]
    first_core = where[1] == 0
    lines, width = keep.shape[1], keep.shape[2]
    tile = 256
    for left in range(0, total.shape[0], tile):
        cut = slice(left, left + tile)
        value = (
            total[cut, :]
            + along_tokens(far_first[:, cut], against[:part])
            + along_tokens(far_second[:, cut], against[part:])
        )
        value = value.reshape(tile // (2 * lines), 2, lines, width)
        even, odd = value[:, 0], value[:, 1]
        out = slice(left // (2 * lines), (left + tile) // (2 * lines))
        keep[out] = jnp.where(first_core, even, odd)
        give[out] = jnp.where(first_core, odd, even).astype(give.dtype)


def shards(features, cotangents, moment_one, moment_two, master, average):
    f32, bf16 = jnp.float32, jnp.bfloat16
    col_width = cotangents.shape[3]
    rows = moment_one.shape[1]
    nx, ny, nr = (lax.axis_size(name) for name in XYR)
    nt = lax.axis_size("tensor")
    peers = nx * ny * nr
    core = lax.axis_index("core")
    twin = lax.axis_index("replica")
    place = lax.axis_index("tensor")
    where = jnp.stack([place, core]).astype(jnp.int32)

    tokens = features[0]
    count, dim_model = tokens.shape
    part = count // 2
    width = 2 * col_width
    up, down = round_trip(nt, 1), round_trip(nt, nt - 1)
    low = lax.ppermute(tokens, "tensor", up)
    high = lax.ppermute(tokens, "tensor", down)

    local = pl.BlockSpec(memory_space=pltpu.VMEM)
    anywhere = pl.BlockSpec(memory_space=pl.ANY)
    state = pl.pallas_call(
        state_kernel,
        out_shape=jax.ShapeDtypeStruct((nx * ny, 4, rows, width), bf16),
        in_specs=[local] * 3,
        out_specs=local,
    )(moment_one, moment_two, master)
    state = lax.all_to_all(state, PLANE, 0, 0, tiled=True)

    far_first = lax.ppermute(low[:part], "tensor", up)
    far_second = lax.ppermute(high[part:], "tensor", down)
    outgrad = cotangents[0].reshape(cotangents.shape[1], 2 * col_width)

    lines = nr * rows
    scalars = pl.BlockSpec(memory_space=pltpu.SMEM)
    params = pltpu.CompilerParams(vmem_limit_bytes=4 * 2**20)
    total = pl.pallas_call(
        near_kernel,
        out_shape=jax.ShapeDtypeStruct((dim_model, width), f32),
        in_specs=[scalars] + [local] * 4,
        out_specs=local,
        compiler_params=params,
        cost_estimate=pl.CostEstimate(
            flops=6 * count * dim_model * width, bytes_accessed=6 * 2**20, transcendentals=0
        ),
    )(where, tokens, low, high, outgrad)
    keep, give = pl.pallas_call(
        far_kernel,
        out_shape=(
            jax.ShapeDtypeStruct((nx * ny, lines, width), f32),
            jax.ShapeDtypeStruct((nx * ny, lines, width), bf16),
        ),
        in_specs=[scalars] + [local] * 4 + [anywhere],
        out_specs=(local, local),
        compiler_params=params,
        cost_estimate=pl.CostEstimate(
            flops=2 * count * dim_model * width, bytes_accessed=6 * 2**20, transcendentals=0
        ),
    )(where, total, far_first, far_second, outgrad, state)

    got = lax.ppermute(give, "core", SWAP)
    half = (keep + got.astype(f32)).astype(bf16).reshape(peers, rows, width)
    terms = lax.all_to_all(half, XYR, split_axis=0, concat_axis=0, tiled=True)
    grad_lines = jnp.sum(terms.astype(f32), axis=0)
    gradient = jnp.transpose(grad_lines.reshape(rows, 2, col_width), (1, 0, 2))

    shared = gather_plane(grad_lines.astype(bf16)).astype(f32)
    squares = jnp.sum(shared * shared, axis=(0, 1)).reshape(2, col_width).sum(axis=0)
    others = ("core", "tensor", "replica")
    squares = jnp.broadcast_to(squares, (lax.axis_size(others), col_width))
    squares = jnp.sum(lax.all_to_all(squares, others, 0, 0, tiled=True))
    count_all = 2.0 * dim_model * dim_model
    clip_factor = 1.0 / jnp.sqrt(squares / count_all + 1e-06)

    fix_one = 1.0 - beta_one**STEP
    fix_two = 1.0 - beta_two**STEP

    def update(grad, one, two, held):
        scaled = clip_factor * grad
        new_one = beta_one * one + (1.0 - beta_one) * scaled
        new_two = beta_two * two + (1.0 - beta_two) * (scaled * scaled)
        direction = new_one / fix_one / (jnp.sqrt(new_two / fix_two) + adam_eps)
        return new_one, new_two, held - learn_rate * (direction + decay_rate * held)

    wide = state.astype(f32)
    mine = update(shared, wide[:, 0], wide[:, 1], wide[:, 2] + wide[:, 3])[2].astype(bf16)
    other = lax.ppermute(mine, "replica", SWAP)
    mine, other = jnp.where(twin == 0, mine, other), jnp.where(twin == 0, other, mine)
    mine = jnp.stack([mine, other], axis=1)
    other = lax.ppermute(mine, "core", SWAP)
    mine, other = jnp.where(core == 0, mine, other), jnp.where(core == 0, other, mine)
    both = jnp.stack([mine, other], axis=1).reshape(nx * ny, 2, nr, rows, 2, col_width)
    weights = jnp.transpose(both, (4, 0, 1, 2, 3, 5)).reshape(2, dim_model, col_width)

    new_first, new_second, new_master = update(gradient, moment_one, moment_two, master)
    flat_rows = new_master.reshape(2 * rows, col_width)
    row_flat = lax.all_to_all(flat_rows, "tensor", split_axis=0, concat_axis=1, tiled=True)
    new_average = average_keep * average + (1.0 - average_keep) * row_flat.reshape(average.shape)
    return (weights, new_first, new_second, new_master, new_average)


def solution(mesh):
    shape = dict(zip(mesh.axis_names, mesh.devices.shape))
    nx, ny = 4, shape["dp"] // 8
    fine = Mesh(
        mesh.devices.reshape(nx, ny, 2, shape["tensor"], shape["replica"]),
        ("x", "y", "core", "tensor", "replica"),
    )
    groups = ("x", "y", "core", "replica")
    state = P(None, groups, "tensor")
    placed = (
        P(groups, "tensor", None),
        P(groups, None, None, "tensor"),
        state,
        state,
        state,
        P(groups, "tensor", None, None),
    )
    return jax.shard_map(
        shards,
        mesh=fine,
        in_specs=placed,
        out_specs=(P(None, None, "tensor"), state, state, state, P(groups, "tensor", None, None)),
        check_vma=False,
    )
```

```python
import jax
import jax.numpy as jnp
from jax import lax
from jax.experimental import pallas as pl
from jax.experimental.pallas import tpu as pltpu
from jax.sharding import Mesh, PartitionSpec as P

STEP = 100


beta_one = 0.9
beta_two = 0.95
learn_rate = 0.05
decay_rate = 0.1
adam_eps = 1e-08
average_keep = 0.9

XYR = ("x", "y", "replica")
SWAP = ((0, 1), (1, 0))


def round_trip(count, step):
    return [(i, (i + step) % count) for i in range(count)]


def along_tokens(block, against):
    return lax.dot_general(
        block, against, (((0,), (0,)), ((), ())), preferred_element_type=jnp.float32
    )


def near_kernel(where, own, low_first, low_second, high_first, high_second, outgrad, total):
    count, part = own.shape[0], low_first.shape[0]
    shards_all = outgrad.shape[0] // count
    tile = 256

    def against(step):
        start = lax.rem(where[0] + step, shards_all) * count
        return outgrad[pl.ds(pl.multiple_of(start, count), count), :]

    for left in range(0, own.shape[1], tile):
        cut = slice(left, left + tile)
        below, above = against(shards_all - 1), against(1)
        total[cut, :] = (
            along_tokens(own[:, cut], against(0))
            + along_tokens(low_first[:, cut], below[:part])
            + along_tokens(low_second[:, cut], below[part:])
            + along_tokens(high_first[:, cut], above[:part])
            + along_tokens(high_second[:, cut], above[part:])
        )


def far_kernel(where, total, far_first, far_second, outgrad, keep, give):
    part = far_first.shape[0]
    start = lax.rem(where[0] + 2, outgrad.shape[0] // (2 * part)) * (2 * part)
    against = outgrad[pl.ds(pl.multiple_of(start, 2 * part), 2 * part), :]
    first_core = where[1] == 0
    lines, width = keep.shape[1], keep.shape[2]
    tile = 256
    for left in range(0, total.shape[0], tile):
        cut = slice(left, left + tile)
        value = (
            total[cut, :]
            + along_tokens(far_first[:, cut], against[:part])
            + along_tokens(far_second[:, cut], against[part:])
        )
        value = value.reshape(tile // (2 * lines), 2, lines, width)
        even, odd = value[:, 0], value[:, 1]
        out = slice(left // (2 * lines), (left + tile) // (2 * lines))
        keep[out] = jnp.where(first_core, even, odd)
        give[out] = jnp.where(first_core, odd, even).astype(give.dtype)


def own_kernel(
    where, lines, sums, one, two, held, new_one, new_two, new_held, spread, *lent
):
    halves, rows, width = one.shape
    peers = spread.shape[0]
    count_all = 2.0 * (width * len(lent)) ** 2
    total = jnp.sum(sums[...], axis=(0, 1), keepdims=True)[0]
    total = jnp.sum(total, axis=1, keepdims=True)
    clip_factor = 1.0 / jnp.sqrt(total / count_all + 1e-06)
    fix_one = 1.0 - beta_one**STEP
    fix_two = 1.0 - beta_two**STEP
    blocks = []
    for half in range(halves):
        scaled = clip_factor * lines[:, half * width : (half + 1) * width]
        first = beta_one * one[half] + (1.0 - beta_one) * scaled
        second = beta_two * two[half] + (1.0 - beta_two) * (scaled * scaled)
        direction = first / fix_one / (jnp.sqrt(second / fix_two) + adam_eps)
        master = held[half] - learn_rate * (direction + decay_rate * held[half])
        new_one[half] = first
        new_two[half] = second
        new_held[half] = master
        copy = master.astype(spread.dtype)
        spread[:, half] = jnp.broadcast_to(copy[None], (peers, rows, width))
        count = halves * rows // len(lent)
        blocks += [master[row : row + count] for row in range(0, rows, count)]
    for step, ref in enumerate(lent):
        target = lax.rem(where[0] + step, len(lent))
        chosen = blocks[0]
        for k in range(1, len(lent)):
            chosen = jnp.where(target == k, blocks[k], chosen)
        ref[...] = chosen


def average_kernel(where, average, *refs):
    *lent, out = refs
    shards_all = len(lent)
    width = lent[0].shape[1]
    for source in range(shards_all):
        step = lax.rem(where[0] + shards_all - source, shards_all)
        chosen = lent[0][...]
        for k in range(1, shards_all):
            chosen = jnp.where(step == k, lent[k][...], chosen)
        columns = slice(source * width, (source + 1) * width)
        kept = average_keep * average[0, 0, :, columns]
        out[0, 0, :, columns] = kept + (1.0 - average_keep) * chosen


def weights_kernel(where, column, other, weights):
    peers, halves, rows, width = column.shape
    lines = weights.shape[1] // peers
    core = where[1]

    def place(ref, pair, half, start):
        pieces = ref[pl.ds(2 * pair, 2), half].astype(jnp.float32)
        pieces = pieces.reshape(2 * rows, width).astype(weights.dtype)
        start = pl.multiple_of(start, 2 * rows)
        weights[half, pl.ds(start, 2 * rows), :] = pieces

    def step(pair, carry):
        for half in range(halves):
            place(column, pair, half, (2 * pair + core) * 2 * rows)
            place(other, pair, half, (2 * pair + 1 - core) * 2 * rows)
        return carry

    lax.fori_loop(0, peers // 2, step, 0, unroll=8)


def shards(features, cotangents, moment_one, moment_two, master, average):
    f32, bf16 = jnp.float32, jnp.bfloat16
    col_width = cotangents.shape[3]
    rows = moment_one.shape[1]
    nx, ny, nr = (lax.axis_size(name) for name in XYR)
    nt = lax.axis_size("tensor")
    peers = nx * ny * nr
    core = lax.axis_index("core")
    place = lax.axis_index("tensor")
    where = jnp.stack([place, core]).astype(jnp.int32)

    tokens = features[0]
    count, dim_model = tokens.shape
    part = count // 2
    first, second = tokens[:part], tokens[part:]
    up, down = round_trip(nt, 1), round_trip(nt, nt - 1)
    low_first = lax.ppermute(first, "tensor", up)
    high_second = lax.ppermute(second, "tensor", down)
    low_second = lax.ppermute(second, "tensor", up)
    high_first = lax.ppermute(first, "tensor", down)
    far_first = lax.ppermute(low_first, "tensor", up)
    far_second = lax.ppermute(high_second, "tensor", down)
    outgrad = cotangents[0].reshape(cotangents.shape[1], 2 * col_width)

    width = 2 * col_width
    lines = nr * rows
    scalars = pl.BlockSpec(memory_space=pltpu.SMEM)
    local = pl.BlockSpec(memory_space=pltpu.VMEM)
    params = pltpu.CompilerParams(vmem_limit_bytes=24 * 2**20)
    total = pl.pallas_call(
        near_kernel,
        out_shape=jax.ShapeDtypeStruct((dim_model, width), f32),
        in_specs=[scalars] + [local] * 6,
        out_specs=local,
        compiler_params=params,
        cost_estimate=pl.CostEstimate(
            flops=6 * count * dim_model * width, bytes_accessed=6 * 2**20, transcendentals=0
        ),
    )(where, tokens, low_first, low_second, high_first, high_second, outgrad)
    keep, give = pl.pallas_call(
        far_kernel,
        out_shape=(
            jax.ShapeDtypeStruct((nx * ny, lines, width), f32),
            jax.ShapeDtypeStruct((nx * ny, lines, width), bf16),
        ),
        in_specs=[scalars] + [local] * 4,
        out_specs=(local, local),
        compiler_params=params,
        cost_estimate=pl.CostEstimate(
            flops=2 * count * dim_model * width, bytes_accessed=6 * 2**20, transcendentals=0
        ),
    )(where, total, far_first, far_second, outgrad)

    got = lax.ppermute(give, "core", SWAP)
    half = (keep + got.astype(f32)).astype(bf16).reshape(peers, rows, width)
    terms = lax.all_to_all(half, XYR, split_axis=0, concat_axis=0, tiled=True)
    grad_lines = jnp.sum(terms.astype(f32), axis=0)
    gradient = grad_lines.reshape(rows, 2, col_width)

    squares = jnp.sum(gradient * gradient, axis=(0, 1))
    for names in (("x", "core", "replica"), ("y", "tensor")):
        spread = jnp.broadcast_to(squares, (lax.axis_size(names), 1, col_width))
        spread = lax.all_to_all(spread, names, 0, 0, tiled=True)
        squares = jnp.sum(spread, axis=(0, 1))

    held_rows = 2 * rows // nt
    piece = jax.ShapeDtypeStruct(moment_one.shape, f32)
    line = jax.ShapeDtypeStruct((held_rows, col_width), f32)
    new_first, new_second, new_master, spread, *lent = pl.pallas_call(
        own_kernel,
        out_shape=(piece, piece, piece)
        + (jax.ShapeDtypeStruct((peers,) + moment_one.shape, bf16),)
        + (line,) * nt,
        in_specs=[scalars] + [local] * 5,
        out_specs=(local,) * (4 + nt),
    )(where, grad_lines, spread, moment_one, moment_two, master)

    column = lax.all_to_all(spread, XYR, split_axis=0, concat_axis=0, tiled=True)
    for step in range(1, nt):
        lent[step] = lax.ppermute(lent[step], "tensor", round_trip(nt, step))
    column, lent = lax.optimization_barrier((column, lent))
    new_average = pl.pallas_call(
        average_kernel,
        out_shape=jax.ShapeDtypeStruct(average.shape, f32),
        in_specs=[scalars] + [local] * (1 + nt),
        out_specs=local,
    )(where, average, *lent)
    other = lax.ppermute(column, "core", SWAP)
    weights = pl.pallas_call(
        weights_kernel,
        out_shape=jax.ShapeDtypeStruct((2, dim_model, col_width), bf16),
        in_specs=[scalars, local, local],
        out_specs=local,
        compiler_params=params,
    )(where, column, other)
    return (weights, new_first, new_second, new_master, new_average)


def solution(mesh):
    shape = dict(zip(mesh.axis_names, mesh.devices.shape))
    nx, ny = 4, shape["dp"] // 8
    fine = Mesh(
        mesh.devices.reshape(nx, ny, 2, shape["tensor"], shape["replica"]),
        ("x", "y", "core", "tensor", "replica"),
    )
    groups = ("x", "y", "core", "replica")
    state = P(None, groups, "tensor")
    placed = (
        P(groups, "tensor", None),
        P(groups, None, None, "tensor"),
        state,
        state,
        state,
        P(groups, "tensor", None, None),
    )
    return jax.shard_map(
        shards,
        mesh=fine,
        in_specs=placed,
        out_specs=(P(None, None, "tensor"), state, state, state, P(groups, "tensor", None, None)),
        check_vma=False,
    )
```

```python
import functools

import jax
import jax.numpy as jnp
from jax import lax
from jax.experimental import pallas as pl
from jax.experimental.pallas import tpu as pltpu
from jax.sharding import Mesh, PartitionSpec as P

STEP = 100


beta_one = 0.9
beta_two = 0.95
learn_rate = 0.05
decay_rate = 0.1
adam_eps = 1e-08
average_keep = 0.9

XYR = ("x", "y", "replica")
PLANE = ("x", "y")
SWAP = ((0, 1), (1, 0))


def round_trip(count, step):
    return [(i, (i + step) % count) for i in range(count)]


def along_tokens(block, against):
    return lax.dot_general(
        block, against, (((0,), (0,)), ((), ())), preferred_element_type=jnp.float32
    )


def near_kernel(where, own, low_first, low_second, high_first, high_second, outgrad, total):
    count, part = own.shape[0], low_first.shape[0]
    shards_all = outgrad.shape[0] // count
    tile = 256

    def against(step):
        start = lax.rem(where[0] + step, shards_all) * count
        return outgrad[pl.ds(pl.multiple_of(start, count), count), :]

    for left in range(0, own.shape[1], tile):
        cut = slice(left, left + tile)
        below, above = against(shards_all - 1), against(1)
        total[cut, :] = (
            along_tokens(own[:, cut], against(0))
            + along_tokens(low_first[:, cut], below[:part])
            + along_tokens(low_second[:, cut], below[part:])
            + along_tokens(high_first[:, cut], above[:part])
            + along_tokens(high_second[:, cut], above[part:])
        )


def far_kernel(where, total, far_first, far_second, outgrad, keep, give):
    part = far_first.shape[0]
    start = lax.rem(where[0] + 2, outgrad.shape[0] // (2 * part)) * (2 * part)
    against = outgrad[pl.ds(pl.multiple_of(start, 2 * part), 2 * part), :]
    first_core = where[1] == 0
    lines, width = keep.shape[1], keep.shape[2]
    tile = 256
    for left in range(0, total.shape[0], tile):
        cut = slice(left, left + tile)
        value = (
            total[cut, :]
            + along_tokens(far_first[:, cut], against[:part])
            + along_tokens(far_second[:, cut], against[part:])
        )
        value = value.reshape(tile // (2 * lines), 2, lines, width)
        even, odd = value[:, 0], value[:, 1]
        out = slice(left // (2 * lines), (left + tile) // (2 * lines))
        keep[out] = jnp.where(first_core, even, odd)
        give[out] = jnp.where(first_core, odd, even).astype(give.dtype)


def row_blocks(lines, count):
    width = lines.shape[1] // 2
    halves = (lines[:, :width], lines[:, width:])
    held = 2 * lines.shape[0] // count
    return [half[row : row + held] for half in halves for row in range(0, lines.shape[0], held)]


def pick(index, blocks):
    chosen = blocks[0]
    for k in range(1, len(blocks)):
        chosen = jnp.where(index == k, blocks[k], chosen)
    return chosen


def whole_lines(ref):
    return jnp.concatenate([ref[0], ref[1]], axis=1)


def state_kernel(where, one, two, held, wide, *lent):
    bf16 = jnp.bfloat16
    parts = (whole_lines(one), whole_lines(two), whole_lines(held))
    high = parts[2].astype(bf16)
    low = (parts[2] - high.astype(jnp.float32)).astype(bf16)
    for k, block in enumerate((parts[0].astype(bf16), parts[1].astype(bf16), high, low)):
        wide[:, k] = jnp.broadcast_to(block[None], (wide.shape[0],) + block.shape)
    for k, block in enumerate(parts):
        blocks = row_blocks(block, len(lent))
        for step, ref in enumerate(lent):
            ref[k] = pick(lax.rem(where[0] + step, len(lent)), blocks)


def clip_of(sums, count):
    total = jnp.sum(sums[:, sums.shape[1] - 1 :, :], axis=(0, 1), keepdims=True)[0]
    total = jnp.sum(total, axis=1, keepdims=True)
    return 1.0 / jnp.sqrt(total / count + 1e-06)


def update(clip_factor, grad, one, two, held):
    fix_one = 1.0 - beta_one**STEP
    fix_two = 1.0 - beta_two**STEP
    scaled = clip_factor * grad
    first = beta_one * one + (1.0 - beta_one) * scaled
    second = beta_two * two + (1.0 - beta_two) * (scaled * scaled)
    direction = first / fix_one / (jnp.sqrt(second / fix_two) + adam_eps)
    return first, second, held - learn_rate * (direction + decay_rate * held)


def plane_kernel(count, sums, shared, state, mine):
    f32 = jnp.float32
    clip_factor = clip_of(sums, count)

    def step(k, carry):
        parts = [state[k, i].astype(f32) for i in range(4)]
        grad = shared[k].astype(f32)
        new = update(clip_factor, grad, parts[0], parts[1], parts[2] + parts[3])[2]
        mine[k] = new.astype(mine.dtype)
        return carry

    lax.fori_loop(0, shared.shape[0], step, 0, unroll=8)


def own_kernel(count, where, sums, lines, one, two, held, average, *refs):
    *lent_state, new_one, new_two, new_held, out = refs
    shards_all = len(lent_state)
    clip_factor = clip_of(sums, count)
    width = one.shape[2]
    for half in range(2):
        grad = lines[:, half * width : (half + 1) * width]
        results = update(clip_factor, grad, one[half], two[half], held[half])
        new_one[half], new_two[half], new_held[half] = results
    for source in range(shards_all):
        step = lax.rem(where[0] + shards_all - source, shards_all)
        state = [pick(step, [ref[k] for ref in lent_state]) for k in range(3)]
        grad = sums[(where[1] * shards_all + source) * 2 + where[2]][: state[0].shape[0]]
        columns = slice(source * width, (source + 1) * width)
        kept = average_keep * average[0, 0, :, columns]
        out[0, 0, :, columns] = kept + (1.0 - average_keep) * update(clip_factor, grad, *state)[2]


def weights_kernel(where, mine, twin, other, other_twin, weights):
    f32 = jnp.float32
    rows, width = mine.shape[1], weights.shape[2]
    core, first = where[1], where[2] == 0

    def place(near, far, start):
        near, far = near.astype(f32), far.astype(f32)
        pieces = [jnp.where(first, near, far), jnp.where(first, far, near)]
        pieces = jnp.concatenate(pieces, axis=0).astype(weights.dtype)
        start = pl.multiple_of(start, 2 * rows)
        weights[0, pl.ds(start, 2 * rows), :] = pieces[:, :width]
        weights[1, pl.ds(start, 2 * rows), :] = pieces[:, width:]

    def step(k, carry):
        place(mine[k], twin[k], (2 * k + core) * 2 * rows)
        place(other[k], other_twin[k], (2 * k + 1 - core) * 2 * rows)
        return carry

    lax.fori_loop(0, mine.shape[0], step, 0, unroll=8)


def shards(features, cotangents, moment_one, moment_two, master, average):
    f32, bf16 = jnp.float32, jnp.bfloat16
    col_width = cotangents.shape[3]
    rows = moment_one.shape[1]
    nx, ny, nr = (lax.axis_size(name) for name in XYR)
    nt = lax.axis_size("tensor")
    peers = nx * ny * nr
    core = lax.axis_index("core")
    place = lax.axis_index("tensor")
    where = jnp.stack([place, core, lax.axis_index("replica")]).astype(jnp.int32)
    ring = lambda blocks: [blocks[0]] + [
        lax.ppermute(blocks[k], "tensor", round_trip(nt, k)) for k in range(1, nt)
    ]

    tokens = features[0]
    count, dim_model = tokens.shape
    part = count // 2
    first, second = tokens[:part], tokens[part:]
    up, down = round_trip(nt, 1), round_trip(nt, nt - 1)
    low_first = lax.ppermute(first, "tensor", up)
    high_second = lax.ppermute(second, "tensor", down)
    low_second = lax.ppermute(second, "tensor", up)
    high_first = lax.ppermute(first, "tensor", down)
    far_first = lax.ppermute(low_first, "tensor", up)
    far_second = lax.ppermute(high_second, "tensor", down)
    outgrad = cotangents[0].reshape(cotangents.shape[1], 2 * col_width)

    scalars = pl.BlockSpec(memory_space=pltpu.SMEM)
    local = pl.BlockSpec(memory_space=pltpu.VMEM)
    params = pltpu.CompilerParams(vmem_limit_bytes=24 * 2**20)

    width = 2 * col_width
    held_rows = 2 * rows // nt
    state, *lent_state = pl.pallas_call(
        state_kernel,
        out_shape=(jax.ShapeDtypeStruct((nx * ny, 4, rows, width), bf16),)
        + (jax.ShapeDtypeStruct((3, held_rows, col_width), f32),) * nt,
        in_specs=[scalars] + [local] * 3,
        out_specs=(local,) * (1 + nt),
    )(where, moment_one, moment_two, master)
    state = lax.all_to_all(state, PLANE, 0, 0, tiled=True)

    lines = nr * rows
    total = pl.pallas_call(
        near_kernel,
        out_shape=jax.ShapeDtypeStruct((dim_model, width), f32),
        in_specs=[scalars] + [local] * 6,
        out_specs=local,
        compiler_params=params,
        cost_estimate=pl.CostEstimate(
            flops=48 * count * dim_model * width, bytes_accessed=6 * 2**20, transcendentals=0
        ),
    )(where, tokens, low_first, low_second, high_first, high_second, outgrad)
    keep, give = pl.pallas_call(
        far_kernel,
        out_shape=(
            jax.ShapeDtypeStruct((nx * ny, lines, width), f32),
            jax.ShapeDtypeStruct((nx * ny, lines, width), bf16),
        ),
        in_specs=[scalars] + [local] * 4,
        out_specs=(local, local),
        compiler_params=params,
        cost_estimate=pl.CostEstimate(
            flops=16 * count * dim_model * width, bytes_accessed=6 * 2**20, transcendentals=0
        ),
    )(where, total, far_first, far_second, outgrad)

    got = lax.ppermute(give, "core", SWAP)
    half = (keep + got.astype(f32)).astype(bf16).reshape(peers, rows, width)
    half, state, lent_state = lax.optimization_barrier((half, state, lent_state))
    terms = lax.all_to_all(half, XYR, split_axis=0, concat_axis=0, tiled=True)
    lent_state = ring(lent_state)
    terms, lent_state = lax.optimization_barrier((terms, lent_state))
    grad_lines = jnp.sum(terms.astype(f32), axis=0)

    spread = grad_lines.astype(bf16)
    spread = jnp.broadcast_to(spread[None], (nx * ny,) + spread.shape)
    shared = lax.all_to_all(spread, PLANE, 0, 0, tiled=True)
    squares = shared.astype(f32)
    squares = jnp.sum(squares * squares, axis=(0, 1))
    squares = squares[:col_width] + squares[col_width:]
    sums = jnp.transpose(grad_lines.reshape(rows, 2, col_width), (1, 0, 2))
    sums = sums.reshape(nt, held_rows, col_width)
    sums = jnp.concatenate([sums, jnp.broadcast_to(squares, sums.shape)], axis=1)
    sums = jnp.broadcast_to(sums[None, :, None], (2, nt, nr) + sums.shape[1:])
    others = ("core", "tensor", "replica")
    sums = lax.all_to_all(
        sums.reshape((2 * nt * nr,) + sums.shape[3:]), others, 0, 0, tiled=True
    )
    count_all = 2.0 * dim_model * dim_model

    mine = pl.pallas_call(
        functools.partial(plane_kernel, count_all),
        out_shape=jax.ShapeDtypeStruct((nx * ny, rows, width), bf16),
        in_specs=[local] * 3,
        out_specs=local,
        compiler_params=params,
    )(sums, shared, state)
    twin = lax.ppermute(mine, "replica", SWAP)
    other = lax.ppermute(mine, "core", SWAP)
    piece = jax.ShapeDtypeStruct(moment_one.shape, f32)
    new_first, new_second, new_master, new_average = pl.pallas_call(
        functools.partial(own_kernel, count_all),
        out_shape=(piece, piece, piece, jax.ShapeDtypeStruct(average.shape, f32)),
        in_specs=[scalars] + [local] * (6 + nt),
        out_specs=(local,) * 4,
    )(
        where, sums, grad_lines, moment_one, moment_two, master, average, *lent_state
    )
    twin, new_average = lax.optimization_barrier((twin, new_average))
    other_twin = lax.ppermute(twin, "core", SWAP)
    weights = pl.pallas_call(
        weights_kernel,
        out_shape=jax.ShapeDtypeStruct((2, dim_model, col_width), bf16),
        in_specs=[scalars] + [local] * 4,
        out_specs=local,
        compiler_params=params,
    )(where, mine, twin, other, other_twin)
    return (weights, new_first, new_second, new_master, new_average)


def solution(mesh):
    shape = dict(zip(mesh.axis_names, mesh.devices.shape))
    nx, ny = 4, shape["dp"] // 8
    fine = Mesh(
        mesh.devices.reshape(nx, ny, 2, shape["tensor"], shape["replica"]),
        ("x", "y", "core", "tensor", "replica"),
    )
    groups = ("x", "y", "core", "replica")
    state = P(None, groups, "tensor")
    placed = (
        P(groups, "tensor", None),
        P(groups, None, None, "tensor"),
        state,
        state,
        state,
        P(groups, "tensor", None, None),
    )
    return jax.shard_map(
        shards,
        mesh=fine,
        in_specs=placed,
        out_specs=(P(None, None, "tensor"), state, state, state, P(groups, "tensor", None, None)),
        check_vma=False,
    )
```

```python
import functools

import jax
import jax.numpy as jnp
from jax import lax
from jax.experimental import pallas as pl
from jax.experimental.pallas import tpu as pltpu
from jax.sharding import Mesh, PartitionSpec as P

STEP = 100


beta_one = 0.9
beta_two = 0.95
learn_rate = 0.05
decay_rate = 0.1
adam_eps = 1e-08
average_keep = 0.9

PEERS = ("y", "replica", "x")
PLANE = ("y", "x")
SWAP = ((0, 1), (1, 0))


def round_trip(count, step):
    return [(i, (i + step) % count) for i in range(count)]


def along_tokens(block, against):
    return lax.dot_general(
        block, against, (((0,), (0,)), ((), ())), preferred_element_type=jnp.float32
    )


def near_kernel(where, own, low_first, low_second, high_first, high_second, outgrad, total):
    count, part = own.shape[0], low_first.shape[0]
    shards_all = outgrad.shape[0] // count
    tile = 256

    def against(step):
        start = lax.rem(where[0] + step, shards_all) * count
        return outgrad[pl.ds(pl.multiple_of(start, count), count), :]

    for left in range(0, own.shape[1], tile):
        cut = slice(left, left + tile)
        below, above = against(shards_all - 1), against(1)
        total[cut, :] = (
            along_tokens(own[:, cut], against(0))
            + along_tokens(low_first[:, cut], below[:part])
            + along_tokens(low_second[:, cut], below[part:])
            + along_tokens(high_first[:, cut], above[:part])
            + along_tokens(high_second[:, cut], above[part:])
        )


def far_kernel(where, total, far_first, far_second, outgrad, keep, give):
    part = far_first.shape[0]
    start = lax.rem(where[0] + 2, outgrad.shape[0] // (2 * part)) * (2 * part)
    against = outgrad[pl.ds(pl.multiple_of(start, 2 * part), 2 * part), :]
    first_core = where[1] == 0
    replicas, columns, rows, width = keep.shape[1:]
    lines = replicas * rows
    tile = total.shape[0] // columns
    for left in range(0, total.shape[0], tile):
        cut = slice(left, left + tile)
        value = (
            total[cut, :]
            + along_tokens(far_first[:, cut], against[:part])
            + along_tokens(far_second[:, cut], against[part:])
        )
        value = value.reshape(tile // (2 * lines), 2, replicas, rows, width)
        even, odd = value[:, 0], value[:, 1]
        keep[:, :, left // tile] = jnp.where(first_core, even, odd)
        give[:, :, left // tile] = jnp.where(first_core, odd, even).astype(give.dtype)


def row_blocks(lines, count):
    width = lines.shape[1] // 2
    halves = (lines[:, :width], lines[:, width:])
    held = 2 * lines.shape[0] // count
    return [half[row : row + held] for half in halves for row in range(0, lines.shape[0], held)]


def pick(index, blocks):
    chosen = blocks[0]
    for k in range(1, len(blocks)):
        chosen = jnp.where(index == k, blocks[k], chosen)
    return chosen


def whole_lines(ref):
    return jnp.concatenate([ref[0], ref[1]], axis=1)


def state_kernel(where, one, two, held, wide, *lent):
    bf16 = jnp.bfloat16
    parts = (whole_lines(one), whole_lines(two), whole_lines(held))
    high = parts[2].astype(bf16)
    low = (parts[2] - high.astype(jnp.float32)).astype(bf16)
    for k, block in enumerate((parts[0].astype(bf16), parts[1].astype(bf16), high, low)):
        wide[:, k] = jnp.broadcast_to(block[None], (wide.shape[0],) + block.shape)
    for k, block in enumerate(parts):
        blocks = row_blocks(block, len(lent))
        for step, ref in enumerate(lent):
            ref[k] = pick(lax.rem(where[0] + step, len(lent)), blocks)


def clip_of(sums, count):
    parts = sums[...].astype(jnp.float32)[:, sums.shape[1] - 4 :, :]
    total = jnp.sum(parts, axis=(0, 1), keepdims=True)[0]
    total = jnp.sum(total, axis=1, keepdims=True)
    return 1.0 / jnp.sqrt(total / count + 1e-06)


def update(clip_factor, grad, one, two, held):
    fix_one = 1.0 - beta_one**STEP
    fix_two = 1.0 - beta_two**STEP
    scaled = clip_factor * grad
    first = beta_one * one + (1.0 - beta_one) * scaled
    second = beta_two * two + (1.0 - beta_two) * (scaled * scaled)
    direction = first / fix_one / (jnp.sqrt(second / fix_two) + adam_eps)
    return first, second, held - learn_rate * (direction + decay_rate * held)


def plane_kernel(count, sums, shared, state, mine):
    f32 = jnp.float32
    clip_factor = clip_of(sums, count)

    def step(k, carry):
        parts = [state[k, i].astype(f32) for i in range(4)]
        grad = shared[k].astype(f32)
        new = update(clip_factor, grad, parts[0], parts[1], parts[2] + parts[3])[2]
        mine[k] = new.astype(mine.dtype)
        return carry

    lax.fori_loop(0, shared.shape[0], step, 0, unroll=8)


def own_kernel(count, where, sums, lines, one, two, held, average, *refs):
    *lent_state, new_one, new_two, new_held, out = refs
    shards_all = len(lent_state)
    clip_factor = clip_of(sums, count)
    width = one.shape[2]
    for half in range(2):
        grad = lines[:, half * width : (half + 1) * width]
        results = update(clip_factor, grad, one[half], two[half], held[half])
        new_one[half], new_two[half], new_held[half] = results
    for source in range(shards_all):
        step = lax.rem(where[0] + shards_all - source, shards_all)
        state = [pick(step, [ref[k] for ref in lent_state]) for k in range(3)]
        grad = sums[(source * 2 + where[2]) * 2 + where[1]].astype(jnp.float32)
        grad = grad[: state[0].shape[0]]
        columns = slice(source * width, (source + 1) * width)
        kept = average_keep * average[0, 0, :, columns]
        out[0, 0, :, columns] = kept + (1.0 - average_keep) * update(clip_factor, grad, *state)[2]


def weights_kernel(columns, where, mine, twin, other, other_twin, weights):
    f32 = jnp.float32
    lines = mine.shape[0] // columns
    rows, width = mine.shape[1], weights.shape[2]
    core, first = where[1], where[2] == 0

    def place(near, far, start):
        near, far = near.astype(f32), far.astype(f32)
        pieces = [jnp.where(first, near, far), jnp.where(first, far, near)]
        pieces = jnp.concatenate(pieces, axis=0).astype(weights.dtype)
        start = pl.multiple_of(start, 2 * rows)
        weights[0, pl.ds(start, 2 * rows), :] = pieces[:, :width]
        weights[1, pl.ds(start, 2 * rows), :] = pieces[:, width:]

    def step(y, carry):
        for x in range(columns):
            k, block = y * columns + x, 2 * (x * lines + y)
            place(mine[k], twin[k], (block + core) * 2 * rows)
            place(other[k], other_twin[k], (block + 1 - core) * 2 * rows)
        return carry

    lax.fori_loop(0, lines, step, 0, unroll=2)


def shards(features, cotangents, moment_one, moment_two, master, average):
    f32, bf16 = jnp.float32, jnp.bfloat16
    col_width = cotangents.shape[3]
    rows = moment_one.shape[1]
    ny, nr, nx = (lax.axis_size(name) for name in PEERS)
    nt = lax.axis_size("tensor")
    peers = nx * ny * nr
    core = lax.axis_index("core")
    place = lax.axis_index("tensor")
    where = jnp.stack([place, core, lax.axis_index("replica")]).astype(jnp.int32)
    ring = lambda blocks: [blocks[0]] + [
        lax.ppermute(blocks[k], "tensor", round_trip(nt, k)) for k in range(1, nt)
    ]

    tokens = features[0]
    count, dim_model = tokens.shape
    part = count // 2
    first, second = tokens[:part], tokens[part:]
    up, down = round_trip(nt, 1), round_trip(nt, nt - 1)
    low_first = lax.ppermute(first, "tensor", up)
    high_second = lax.ppermute(second, "tensor", down)
    low_second = lax.ppermute(second, "tensor", up)
    high_first = lax.ppermute(first, "tensor", down)
    far_first = lax.ppermute(low_first, "tensor", up)
    far_second = lax.ppermute(high_second, "tensor", down)
    outgrad = cotangents[0].reshape(cotangents.shape[1], 2 * col_width)

    scalars = pl.BlockSpec(memory_space=pltpu.SMEM)
    local = pl.BlockSpec(memory_space=pltpu.VMEM)
    params = pltpu.CompilerParams(vmem_limit_bytes=24 * 2**20)

    width = 2 * col_width
    held_rows = 2 * rows // nt
    state, *lent_state = pl.pallas_call(
        state_kernel,
        out_shape=(jax.ShapeDtypeStruct((nx * ny, 4, rows, width), bf16),)
        + (jax.ShapeDtypeStruct((3, held_rows, col_width), f32),) * nt,
        in_specs=[scalars] + [local] * 3,
        out_specs=(local,) * (1 + nt),
    )(where, moment_one, moment_two, master)
    state = lax.all_to_all(state, PLANE, 0, 0, tiled=True)

    total = pl.pallas_call(
        near_kernel,
        out_shape=jax.ShapeDtypeStruct((dim_model, width), f32),
        in_specs=[scalars] + [local] * 6,
        out_specs=local,
        compiler_params=params,
        cost_estimate=pl.CostEstimate(
            flops=48 * count * dim_model * width, bytes_accessed=6 * 2**20, transcendentals=0
        ),
    )(where, tokens, low_first, low_second, high_first, high_second, outgrad)
    keep, give = pl.pallas_call(
        far_kernel,
        out_shape=(
            jax.ShapeDtypeStruct((ny, nr, nx, rows, width), f32),
            jax.ShapeDtypeStruct((ny, nr, nx, rows, width), bf16),
        ),
        in_specs=[scalars] + [local] * 4,
        out_specs=(local, local),
        compiler_params=params,
        cost_estimate=pl.CostEstimate(
            flops=16 * count * dim_model * width, bytes_accessed=6 * 2**20, transcendentals=0
        ),
    )(where, total, far_first, far_second, outgrad)

    got = lax.ppermute(give, "core", SWAP)
    half = (keep + got.astype(f32)).astype(bf16).reshape(peers, rows, width)
    half, state, lent_state = lax.optimization_barrier((half, state, lent_state))
    terms = lax.all_to_all(half, PEERS, split_axis=0, concat_axis=0, tiled=True)
    lent_state = ring(lent_state)
    terms, lent_state = lax.optimization_barrier((terms, lent_state))
    grad_lines = jnp.sum(terms.astype(f32), axis=0)

    spread = grad_lines.astype(bf16)
    spread = jnp.broadcast_to(spread[None], (nx * ny,) + spread.shape)
    shared = lax.all_to_all(spread, PLANE, 0, 0, tiled=True)
    shared, lines_after = lax.optimization_barrier((shared, grad_lines))
    squares = shared.astype(f32)
    squares = jnp.sum(squares * squares, axis=(0, 1))
    squares = squares[:col_width] + squares[col_width:]
    high = lax.reduce_precision(squares, 8, 7)
    middle = lax.reduce_precision(squares - high, 8, 7)
    squares = jnp.stack([high, middle, squares - high - middle, jnp.zeros_like(squares)])
    sums = jnp.transpose(lines_after.reshape(rows, 2, col_width), (1, 0, 2))
    sums = sums.reshape(nt, held_rows, col_width)
    squares = jnp.broadcast_to(squares[None], (nt,) + squares.shape)
    sums = jnp.concatenate([sums, squares], axis=1).astype(bf16)
    sums = jnp.broadcast_to(sums[:, None, None], (nt, nr, 2) + sums.shape[1:])
    others = ("tensor", "replica", "core")
    sums = lax.all_to_all(
        sums.reshape((2 * nt * nr,) + sums.shape[3:]), others, 0, 0, tiled=True
    )
    count_all = 2.0 * dim_model * dim_model

    mine = pl.pallas_call(
        functools.partial(plane_kernel, count_all),
        out_shape=jax.ShapeDtypeStruct((nx * ny, rows, width), bf16),
        in_specs=[local] * 3,
        out_specs=local,
        compiler_params=params,
    )(sums, shared, state)
    twin = lax.ppermute(mine, "replica", SWAP)
    other = lax.ppermute(mine, "core", SWAP)
    piece = jax.ShapeDtypeStruct(moment_one.shape, f32)
    new_first, new_second, new_master, new_average = pl.pallas_call(
        functools.partial(own_kernel, count_all),
        out_shape=(piece, piece, piece, jax.ShapeDtypeStruct(average.shape, f32)),
        in_specs=[scalars] + [local] * (6 + nt),
        out_specs=(local,) * 4,
    )(
        where, sums, grad_lines, moment_one, moment_two, master, average, *lent_state
    )
    twin, new_average = lax.optimization_barrier((twin, new_average))
    other_twin = lax.ppermute(twin, "core", SWAP)
    weights = pl.pallas_call(
        functools.partial(weights_kernel, nx),
        out_shape=jax.ShapeDtypeStruct((2, dim_model, col_width), bf16),
        in_specs=[scalars] + [local] * 4,
        out_specs=local,
        compiler_params=params,
    )(where, mine, twin, other, other_twin)
    return (weights, new_first, new_second, new_master, new_average)


def solution(mesh):
    shape = dict(zip(mesh.axis_names, mesh.devices.shape))
    nx, ny = 4, shape["dp"] // 8
    fine = Mesh(
        mesh.devices.reshape(nx, ny, 2, shape["tensor"], shape["replica"]),
        ("x", "y", "core", "tensor", "replica"),
    )
    groups = ("x", "y", "core", "replica")
    state = P(None, groups, "tensor")
    placed = (
        P(groups, "tensor", None),
        P(groups, None, None, "tensor"),
        state,
        state,
        state,
        P(groups, "tensor", None, None),
    )
    return jax.shard_map(
        shards,
        mesh=fine,
        in_specs=placed,
        out_specs=(P(None, None, "tensor"), state, state, state, P(groups, "tensor", None, None)),
        check_vma=False,
    )
```

```python
import functools

import jax
import jax.numpy as jnp
from jax import lax
from jax.experimental import pallas as pl
from jax.experimental.pallas import tpu as pltpu
from jax.sharding import Mesh, PartitionSpec as P

STEP = 100


beta_one = 0.9
beta_two = 0.95
learn_rate = 0.05
decay_rate = 0.1
adam_eps = 1e-08
average_keep = 0.9

PEERS = ("y", "replica", "x")
PLANE = ("y", "x")
SWAP = ((0, 1), (1, 0))


def round_trip(count, step):
    return [(i, (i + step) % count) for i in range(count)]


def along_tokens(block, against):
    return lax.dot_general(
        block, against, (((0,), (0,)), ((), ())), preferred_element_type=jnp.float32
    )


def near_kernel(where, own, low_first, low_second, high_first, high_second, outgrad, total):
    count, part = own.shape[0], low_first.shape[0]
    shards_all = outgrad.shape[0] // count
    tile = 256

    def against(step):
        start = lax.rem(where[0] + step, shards_all) * count
        return outgrad[pl.ds(pl.multiple_of(start, count), count), :]

    for left in range(0, own.shape[1], tile):
        cut = slice(left, left + tile)
        below, above = against(shards_all - 1), against(1)
        total[cut, :] = (
            along_tokens(own[:, cut], against(0))
            + along_tokens(low_first[:, cut], below[:part])
            + along_tokens(low_second[:, cut], below[part:])
            + along_tokens(high_first[:, cut], above[:part])
            + along_tokens(high_second[:, cut], above[part:])
        )


def far_kernel(where, total, far_first, far_second, outgrad, keep, give):
    part = far_first.shape[0]
    start = lax.rem(where[0] + 2, outgrad.shape[0] // (2 * part)) * (2 * part)
    against = outgrad[pl.ds(pl.multiple_of(start, 2 * part), 2 * part), :]
    first_core = where[1] == 0
    replicas, columns, rows, width = keep.shape[1:]
    lines = replicas * rows
    tile = total.shape[0] // columns
    for left in range(0, total.shape[0], tile):
        cut = slice(left, left + tile)
        value = (
            total[cut, :]
            + along_tokens(far_first[:, cut], against[:part])
            + along_tokens(far_second[:, cut], against[part:])
        )
        value = value.reshape(tile // (2 * lines), 2, replicas, rows, width)
        even, odd = value[:, 0], value[:, 1]
        keep[:, :, left // tile] = jnp.where(first_core, even, odd)
        give[:, :, left // tile] = jnp.where(first_core, odd, even).astype(give.dtype)


def row_blocks(lines, count):
    width = lines.shape[1] // 2
    halves = (lines[:, :width], lines[:, width:])
    held = 2 * lines.shape[0] // count
    return [half[row : row + held] for half in halves for row in range(0, lines.shape[0], held)]


def pick(index, blocks):
    chosen = blocks[0]
    for k in range(1, len(blocks)):
        chosen = jnp.where(index == k, blocks[k], chosen)
    return chosen


def whole_lines(ref):
    return jnp.concatenate([ref[0], ref[1]], axis=1)


def state_kernel(where, one, two, held, wide, *lent):
    bf16 = jnp.bfloat16
    parts = (whole_lines(one), whole_lines(two), whole_lines(held))
    high = parts[2].astype(bf16)
    low = (parts[2] - high.astype(jnp.float32)).astype(bf16)
    for k, block in enumerate((parts[0].astype(bf16), parts[1].astype(bf16), high, low)):
        wide[:, k] = jnp.broadcast_to(block[None], (wide.shape[0],) + block.shape)
    for k, block in enumerate(parts):
        blocks = row_blocks(block, len(lent))
        for step, ref in enumerate(lent):
            ref[k] = pick(lax.rem(where[0] + step, len(lent)), blocks)


def clip_of(sums, count):
    parts = sums[...].astype(jnp.float32)[:, sums.shape[1] - 4 :, :]
    total = jnp.sum(parts, axis=(0, 1), keepdims=True)[0]
    total = jnp.sum(total, axis=1, keepdims=True)
    return 1.0 / jnp.sqrt(total / count + 1e-06)


def update(clip_factor, grad, one, two, held):
    fix_one = 1.0 - beta_one**STEP
    fix_two = 1.0 - beta_two**STEP
    scaled = clip_factor * grad
    first = beta_one * one + (1.0 - beta_one) * scaled
    second = beta_two * two + (1.0 - beta_two) * (scaled * scaled)
    direction = first / fix_one / (jnp.sqrt(second / fix_two) + adam_eps)
    return first, second, held - learn_rate * (direction + decay_rate * held)


def plane_kernel(count, sums, shared, state, mine):
    f32 = jnp.float32
    clip_factor = clip_of(sums, count)

    def step(k, carry):
        parts = [state[k, i].astype(f32) for i in range(4)]
        grad = shared[k].astype(f32)
        new = update(clip_factor, grad, parts[0], parts[1], parts[2] + parts[3])[2]
        mine[k] = new.astype(mine.dtype)
        return carry

    lax.fori_loop(0, shared.shape[0], step, 0, unroll=8)


def own_kernel(count, where, sums, lines, one, two, held, average, *refs):
    *lent_state, new_one, new_two, new_held, out = refs
    shards_all = len(lent_state)
    clip_factor = clip_of(sums, count)
    width = one.shape[2]
    for half in range(2):
        grad = lines[:, half * width : (half + 1) * width]
        results = update(clip_factor, grad, one[half], two[half], held[half])
        new_one[half], new_two[half], new_held[half] = results
    for source in range(shards_all):
        step = lax.rem(where[0] + shards_all - source, shards_all)
        state = [pick(step, [ref[k] for ref in lent_state]) for k in range(3)]
        grad = sums[(source * 2 + where[2]) * 2 + where[1]].astype(jnp.float32)
        grad = grad[: state[0].shape[0]]
        columns = slice(source * width, (source + 1) * width)
        kept = average_keep * average[0, 0, :, columns]
        out[0, 0, :, columns] = kept + (1.0 - average_keep) * update(clip_factor, grad, *state)[2]


def weights_kernel(columns, where, mine, twin, other, other_twin, weights):
    f32 = jnp.float32
    lines = mine.shape[0] // columns
    rows, width = mine.shape[1], weights.shape[2]
    core, first = where[1], where[2] == 0

    def place(near, far, start):
        near, far = near.astype(f32), far.astype(f32)
        pieces = [jnp.where(first, near, far), jnp.where(first, far, near)]
        pieces = jnp.concatenate(pieces, axis=0).astype(weights.dtype)
        start = pl.multiple_of(start, 2 * rows)
        weights[0, pl.ds(start, 2 * rows), :] = pieces[:, :width]
        weights[1, pl.ds(start, 2 * rows), :] = pieces[:, width:]

    def step(y, carry):
        for x in range(columns):
            k, block = y * columns + x, 2 * (x * lines + y)
            place(mine[k], twin[k], (block + core) * 2 * rows)
            place(other[k], other_twin[k], (block + 1 - core) * 2 * rows)
        return carry

    lax.fori_loop(0, lines, step, 0, unroll=2)


def shards(features, cotangents, moment_one, moment_two, master, average):
    f32, bf16 = jnp.float32, jnp.bfloat16
    col_width = cotangents.shape[3]
    rows = moment_one.shape[1]
    ny, nr, nx = (lax.axis_size(name) for name in PEERS)
    nt = lax.axis_size("tensor")
    peers = nx * ny * nr
    core = lax.axis_index("core")
    place = lax.axis_index("tensor")
    where = jnp.stack([place, core, lax.axis_index("replica")]).astype(jnp.int32)

    tokens = features[0]
    count, dim_model = tokens.shape
    part = count // 2
    first, second = tokens[:part], tokens[part:]
    up, down = round_trip(nt, 1), round_trip(nt, nt - 1)
    low_first = lax.ppermute(first, "tensor", up)
    high_second = lax.ppermute(second, "tensor", down)
    low_second = lax.ppermute(second, "tensor", up)
    high_first = lax.ppermute(first, "tensor", down)
    far_first = lax.ppermute(low_first, "tensor", up)
    far_second = lax.ppermute(high_second, "tensor", down)
    outgrad = cotangents[0].reshape(cotangents.shape[1], 2 * col_width)

    scalars = pl.BlockSpec(memory_space=pltpu.SMEM)
    local = pl.BlockSpec(memory_space=pltpu.VMEM)
    params = pltpu.CompilerParams(vmem_limit_bytes=24 * 2**20)

    width = 2 * col_width
    held_rows = 2 * rows // nt
    state, *lent_state = pl.pallas_call(
        state_kernel,
        out_shape=(jax.ShapeDtypeStruct((nx * ny, 4, rows, width), bf16),)
        + (jax.ShapeDtypeStruct((3, held_rows, col_width), f32),) * nt,
        in_specs=[scalars] + [local] * 3,
        out_specs=(local,) * (1 + nt),
    )(where, moment_one, moment_two, master)
    state = lax.all_to_all(state, PLANE, 0, 0, tiled=True)

    total = pl.pallas_call(
        near_kernel,
        out_shape=jax.ShapeDtypeStruct((dim_model, width), f32),
        in_specs=[scalars] + [local] * 6,
        out_specs=local,
        compiler_params=params,
        cost_estimate=pl.CostEstimate(
            flops=48 * count * dim_model * width, bytes_accessed=6 * 2**20, transcendentals=0
        ),
    )(where, tokens, low_first, low_second, high_first, high_second, outgrad)
    keep, give = pl.pallas_call(
        far_kernel,
        out_shape=(
            jax.ShapeDtypeStruct((ny, nr, nx, rows, width), f32),
            jax.ShapeDtypeStruct((ny, nr, nx, rows, width), bf16),
        ),
        in_specs=[scalars] + [local] * 4,
        out_specs=(local, local),
        compiler_params=params,
        cost_estimate=pl.CostEstimate(
            flops=16 * count * dim_model * width, bytes_accessed=6 * 2**20, transcendentals=0
        ),
    )(where, total, far_first, far_second, outgrad)

    got = lax.ppermute(give, "core", SWAP)
    half = (keep + got.astype(f32)).astype(bf16).reshape(peers, rows, width)
    half, state, lent_state = lax.optimization_barrier((half, state, lent_state))
    terms = lax.all_to_all(half, PEERS, split_axis=0, concat_axis=0, tiled=True)
    for step in range(1, nt - 1):
        lent_state[step] = lax.ppermute(lent_state[step], "tensor", round_trip(nt, step))
    terms, lent_state = lax.optimization_barrier((terms, lent_state))
    grad_lines = jnp.sum(terms.astype(f32), axis=0)

    spread = grad_lines.astype(bf16)
    spread = jnp.broadcast_to(spread[None], (nx * ny,) + spread.shape)
    shared = lax.all_to_all(spread, PLANE, 0, 0, tiled=True)
    lent_state[-1] = lax.ppermute(lent_state[-1], "tensor", round_trip(nt, nt - 1))
    shared, lines_after, lent_state = lax.optimization_barrier((shared, grad_lines, lent_state))
    squares = shared.astype(f32)
    squares = jnp.sum(squares * squares, axis=(0, 1))
    squares = squares[:col_width] + squares[col_width:]
    high = lax.reduce_precision(squares, 8, 7)
    middle = lax.reduce_precision(squares - high, 8, 7)
    squares = jnp.stack([high, middle, squares - high - middle, jnp.zeros_like(squares)])
    sums = jnp.transpose(lines_after.reshape(rows, 2, col_width), (1, 0, 2))
    sums = sums.reshape(nt, held_rows, col_width)
    squares = jnp.broadcast_to(squares[None], (nt,) + squares.shape)
    sums = jnp.concatenate([sums, squares], axis=1).astype(bf16)
    sums = jnp.broadcast_to(sums[:, None, None], (nt, nr, 2) + sums.shape[1:])
    others = ("tensor", "replica", "core")
    sums = lax.all_to_all(
        sums.reshape((2 * nt * nr,) + sums.shape[3:]), others, 0, 0, tiled=True
    )
    count_all = 2.0 * dim_model * dim_model

    mine = pl.pallas_call(
        functools.partial(plane_kernel, count_all),
        out_shape=jax.ShapeDtypeStruct((nx * ny, rows, width), bf16),
        in_specs=[local] * 3,
        out_specs=local,
        compiler_params=params,
    )(sums, shared, state)
    twin = lax.ppermute(mine, "replica", SWAP)
    other = lax.ppermute(mine, "core", SWAP)
    piece = jax.ShapeDtypeStruct(moment_one.shape, f32)
    new_first, new_second, new_master, new_average = pl.pallas_call(
        functools.partial(own_kernel, count_all),
        out_shape=(piece, piece, piece, jax.ShapeDtypeStruct(average.shape, f32)),
        in_specs=[scalars] + [local] * (6 + nt),
        out_specs=(local,) * 4,
    )(
        where, sums, grad_lines, moment_one, moment_two, master, average, *lent_state
    )
    twin, new_average = lax.optimization_barrier((twin, new_average))
    other_twin = lax.ppermute(twin, "core", SWAP)
    weights = pl.pallas_call(
        functools.partial(weights_kernel, nx),
        out_shape=jax.ShapeDtypeStruct((2, dim_model, col_width), bf16),
        in_specs=[scalars] + [local] * 4,
        out_specs=local,
        compiler_params=params,
    )(where, mine, twin, other, other_twin)
    return (weights, new_first, new_second, new_master, new_average)


def solution(mesh):
    shape = dict(zip(mesh.axis_names, mesh.devices.shape))
    nx, ny = 4, shape["dp"] // 8
    fine = Mesh(
        mesh.devices.reshape(nx, ny, 2, shape["tensor"], shape["replica"]),
        ("x", "y", "core", "tensor", "replica"),
    )
    groups = ("x", "y", "core", "replica")
    state = P(None, groups, "tensor")
    placed = (
        P(groups, "tensor", None),
        P(groups, None, None, "tensor"),
        state,
        state,
        state,
        P(groups, "tensor", None, None),
    )
    return jax.shard_map(
        shards,
        mesh=fine,
        in_specs=placed,
        out_specs=(P(None, None, "tensor"), state, state, state, P(groups, "tensor", None, None)),
        check_vma=False,
    )
```

```python
import functools

import jax
import jax.numpy as jnp
from jax import lax
from jax.experimental import pallas as pl
from jax.experimental.pallas import tpu as pltpu
from jax.sharding import Mesh, PartitionSpec as P

STEP = 100


beta_one = 0.9
beta_two = 0.95
learn_rate = 0.05
decay_rate = 0.1
adam_eps = 1e-08
average_keep = 0.9

XYR = ("x", "y", "replica")
PLANE = ("x", "y")
SWAP = ((0, 1), (1, 0))


def round_trip(count, step):
    return [(i, (i + step) % count) for i in range(count)]


def along_tokens(block, against):
    return lax.dot_general(
        block, against, (((0,), (0,)), ((), ())), preferred_element_type=jnp.float32
    )


def near_kernel(where, own, low_first, low_second, high_first, high_second, outgrad, total):
    count, part = own.shape[0], low_first.shape[0]
    shards_all = outgrad.shape[0] // count
    tile = 256

    def against(step):
        start = lax.rem(where[0] + step, shards_all) * count
        return outgrad[pl.ds(pl.multiple_of(start, count), count), :]

    for left in range(0, own.shape[1], tile):
        cut = slice(left, left + tile)
        below, above = against(shards_all - 1), against(1)
        total[cut, :] = (
            along_tokens(own[:, cut], against(0))
            + along_tokens(low_first[:, cut], below[:part])
            + along_tokens(low_second[:, cut], below[part:])
            + along_tokens(high_first[:, cut], above[:part])
            + along_tokens(high_second[:, cut], above[part:])
        )


def far_kernel(where, total, far_first, far_second, outgrad, keep, give):
    part = far_first.shape[0]
    start = lax.rem(where[0] + 2, outgrad.shape[0] // (2 * part)) * (2 * part)
    against = outgrad[pl.ds(pl.multiple_of(start, 2 * part), 2 * part), :]
    first_core = where[1] == 0
    lines, width = keep.shape[1], keep.shape[2]
    tile = 256
    for left in range(0, total.shape[0], tile):
        cut = slice(left, left + tile)
        value = (
            total[cut, :]
            + along_tokens(far_first[:, cut], against[:part])
            + along_tokens(far_second[:, cut], against[part:])
        )
        value = value.reshape(tile // (2 * lines), 2, lines, width)
        even, odd = value[:, 0], value[:, 1]
        out = slice(left // (2 * lines), (left + tile) // (2 * lines))
        keep[out] = jnp.where(first_core, even, odd)
        give[out] = jnp.where(first_core, odd, even).astype(give.dtype)


def row_blocks(lines, count):
    width = lines.shape[1] // 2
    halves = (lines[:, :width], lines[:, width:])
    held = 2 * lines.shape[0] // count
    return [half[row : row + held] for half in halves for row in range(0, lines.shape[0], held)]


def pick(index, blocks):
    chosen = blocks[0]
    for k in range(1, len(blocks)):
        chosen = jnp.where(index == k, blocks[k], chosen)
    return chosen


def whole_lines(ref):
    return jnp.concatenate([ref[0], ref[1]], axis=1)


def state_kernel(where, one, two, held, wide, *lent):
    bf16 = jnp.bfloat16
    parts = (whole_lines(one), whole_lines(two), whole_lines(held))
    high = parts[2].astype(bf16)
    low = (parts[2] - high.astype(jnp.float32)).astype(bf16)
    for k, block in enumerate((parts[0].astype(bf16), parts[1].astype(bf16), high, low)):
        wide[:, k] = jnp.broadcast_to(block[None], (wide.shape[0],) + block.shape)
    for k, block in enumerate(parts):
        blocks = row_blocks(block, len(lent))
        for step, ref in enumerate(lent):
            ref[k] = pick(lax.rem(where[0] + step, len(lent)), blocks)


def clip_of(sums, count):
    parts = sums[...].astype(jnp.float32)[:, sums.shape[1] - 4 :, :]
    total = jnp.sum(parts, axis=(0, 1), keepdims=True)[0]
    total = jnp.sum(total, axis=1, keepdims=True)
    return 1.0 / jnp.sqrt(total / count + 1e-06)


def update(clip_factor, grad, one, two, held):
    fix_one = 1.0 - beta_one**STEP
    fix_two = 1.0 - beta_two**STEP
    scaled = clip_factor * grad
    first = beta_one * one + (1.0 - beta_one) * scaled
    second = beta_two * two + (1.0 - beta_two) * (scaled * scaled)
    direction = first / fix_one / (jnp.sqrt(second / fix_two) + adam_eps)
    return first, second, held - learn_rate * (direction + decay_rate * held)


def plane_kernel(count, sums, shared, state, mine):
    f32 = jnp.float32
    clip_factor = clip_of(sums, count)

    def step(k, carry):
        parts = [state[k, i].astype(f32) for i in range(4)]
        grad = shared[k].astype(f32)
        new = update(clip_factor, grad, parts[0], parts[1], parts[2] + parts[3])[2]
        mine[k] = new.astype(mine.dtype)
        return carry

    lax.fori_loop(0, shared.shape[0], step, 0, unroll=8)


def own_kernel(count, where, sums, lines, one, two, held, average, *refs):
    *lent_state, new_one, new_two, new_held, out = refs
    shards_all = len(lent_state)
    clip_factor = clip_of(sums, count)
    width = one.shape[2]
    for half in range(2):
        grad = lines[:, half * width : (half + 1) * width]
        results = update(clip_factor, grad, one[half], two[half], held[half])
        new_one[half], new_two[half], new_held[half] = results
    for source in range(shards_all):
        step = lax.rem(where[0] + shards_all - source, shards_all)
        state = [pick(step, [ref[k] for ref in lent_state]) for k in range(3)]
        grad = sums[(where[1] * shards_all + source) * 2 + where[2]].astype(jnp.float32)
        grad = grad[: state[0].shape[0]]
        columns = slice(source * width, (source + 1) * width)
        kept = average_keep * average[0, 0, :, columns]
        out[0, 0, :, columns] = kept + (1.0 - average_keep) * update(clip_factor, grad, *state)[2]


def weights_kernel(where, mine, twin, other, other_twin, weights):
    f32 = jnp.float32
    rows, width = mine.shape[1], weights.shape[2]
    core, first = where[1], where[2] == 0

    def place(near, far, start):
        near, far = near.astype(f32), far.astype(f32)
        pieces = [jnp.where(first, near, far), jnp.where(first, far, near)]
        pieces = jnp.concatenate(pieces, axis=0).astype(weights.dtype)
        start = pl.multiple_of(start, 2 * rows)
        weights[0, pl.ds(start, 2 * rows), :] = pieces[:, :width]
        weights[1, pl.ds(start, 2 * rows), :] = pieces[:, width:]

    def step(k, carry):
        place(mine[k], twin[k], (2 * k + core) * 2 * rows)
        place(other[k], other_twin[k], (2 * k + 1 - core) * 2 * rows)
        return carry

    lax.fori_loop(0, mine.shape[0], step, 0, unroll=8)


def shards(features, cotangents, moment_one, moment_two, master, average):
    f32, bf16 = jnp.float32, jnp.bfloat16
    col_width = cotangents.shape[3]
    rows = moment_one.shape[1]
    nx, ny, nr = (lax.axis_size(name) for name in XYR)
    nt = lax.axis_size("tensor")
    peers = nx * ny * nr
    core = lax.axis_index("core")
    place = lax.axis_index("tensor")
    where = jnp.stack([place, core, lax.axis_index("replica")]).astype(jnp.int32)

    tokens = features[0]
    count, dim_model = tokens.shape
    part = count // 2
    first, second = tokens[:part], tokens[part:]
    up, down = round_trip(nt, 1), round_trip(nt, nt - 1)
    low_first = lax.ppermute(first, "tensor", up)
    high_second = lax.ppermute(second, "tensor", down)
    low_second = lax.ppermute(second, "tensor", up)
    high_first = lax.ppermute(first, "tensor", down)
    far_first = lax.ppermute(low_first, "tensor", up)
    far_second = lax.ppermute(high_second, "tensor", down)
    outgrad = cotangents[0].reshape(cotangents.shape[1], 2 * col_width)

    scalars = pl.BlockSpec(memory_space=pltpu.SMEM)
    local = pl.BlockSpec(memory_space=pltpu.VMEM)
    params = pltpu.CompilerParams(vmem_limit_bytes=24 * 2**20)

    width = 2 * col_width
    held_rows = 2 * rows // nt
    state, *lent_state = pl.pallas_call(
        state_kernel,
        out_shape=(jax.ShapeDtypeStruct((nx * ny, 4, rows, width), bf16),)
        + (jax.ShapeDtypeStruct((3, held_rows, col_width), f32),) * nt,
        in_specs=[scalars] + [local] * 3,
        out_specs=(local,) * (1 + nt),
    )(where, moment_one, moment_two, master)
    state = lax.all_to_all(state, PLANE, 0, 0, tiled=True)

    lines = nr * rows
    total = pl.pallas_call(
        near_kernel,
        out_shape=jax.ShapeDtypeStruct((dim_model, width), f32),
        in_specs=[scalars] + [local] * 6,
        out_specs=local,
        compiler_params=params,
        cost_estimate=pl.CostEstimate(
            flops=48 * count * dim_model * width, bytes_accessed=6 * 2**20, transcendentals=0
        ),
    )(where, tokens, low_first, low_second, high_first, high_second, outgrad)
    keep, give = pl.pallas_call(
        far_kernel,
        out_shape=(
            jax.ShapeDtypeStruct((nx * ny, lines, width), f32),
            jax.ShapeDtypeStruct((nx * ny, lines, width), bf16),
        ),
        in_specs=[scalars] + [local] * 4,
        out_specs=(local, local),
        compiler_params=params,
        cost_estimate=pl.CostEstimate(
            flops=16 * count * dim_model * width, bytes_accessed=6 * 2**20, transcendentals=0
        ),
    )(where, total, far_first, far_second, outgrad)

    got = lax.ppermute(give, "core", SWAP)
    half = (keep + got.astype(f32)).astype(bf16).reshape(peers, rows, width)
    half, state, lent_state = lax.optimization_barrier((half, state, lent_state))
    terms = lax.all_to_all(half, XYR, split_axis=0, concat_axis=0, tiled=True)
    for step in range(1, nt - 1):
        lent_state[step] = lax.ppermute(lent_state[step], "tensor", round_trip(nt, step))
    terms, lent_state = lax.optimization_barrier((terms, lent_state))
    grad_lines = jnp.sum(terms.astype(f32), axis=0)

    spread = grad_lines.astype(bf16)
    spread = jnp.broadcast_to(spread[None], (nx * ny,) + spread.shape)
    shared = lax.all_to_all(spread, PLANE, 0, 0, tiled=True)
    lent_state[-1] = lax.ppermute(lent_state[-1], "tensor", round_trip(nt, nt - 1))
    shared, lines_after, lent_state = lax.optimization_barrier((shared, grad_lines, lent_state))
    squares = shared.astype(f32)
    squares = jnp.sum(squares * squares, axis=(0, 1))
    squares = squares[:col_width] + squares[col_width:]
    high = lax.reduce_precision(squares, 8, 7)
    middle = lax.reduce_precision(squares - high, 8, 7)
    squares = jnp.stack([high, middle, squares - high - middle, jnp.zeros_like(squares)])
    sums = jnp.transpose(lines_after.reshape(rows, 2, col_width), (1, 0, 2))
    sums = sums.reshape(nt, held_rows, col_width)
    squares = jnp.broadcast_to(squares[None], (nt,) + squares.shape)
    sums = jnp.concatenate([sums, squares], axis=1).astype(bf16)
    sums = jnp.broadcast_to(sums[None, :, None], (2, nt, nr) + sums.shape[1:])
    others = ("core", "tensor", "replica")
    sums = lax.all_to_all(
        sums.reshape((2 * nt * nr,) + sums.shape[3:]), others, 0, 0, tiled=True
    )
    count_all = 2.0 * dim_model * dim_model

    mine = pl.pallas_call(
        functools.partial(plane_kernel, count_all),
        out_shape=jax.ShapeDtypeStruct((nx * ny, rows, width), bf16),
        in_specs=[local] * 3,
        out_specs=local,
        compiler_params=params,
    )(sums, shared, state)
    twin = lax.ppermute(mine, "replica", SWAP)
    other = lax.ppermute(mine, "core", SWAP)
    piece = jax.ShapeDtypeStruct(moment_one.shape, f32)
    new_first, new_second, new_master, new_average = pl.pallas_call(
        functools.partial(own_kernel, count_all),
        out_shape=(piece, piece, piece, jax.ShapeDtypeStruct(average.shape, f32)),
        in_specs=[scalars] + [local] * (6 + nt),
        out_specs=(local,) * 4,
    )(
        where, sums, grad_lines, moment_one, moment_two, master, average, *lent_state
    )
    twin, new_average = lax.optimization_barrier((twin, new_average))
    other_twin = lax.ppermute(twin, "core", SWAP)
    weights = pl.pallas_call(
        weights_kernel,
        out_shape=jax.ShapeDtypeStruct((2, dim_model, col_width), bf16),
        in_specs=[scalars] + [local] * 4,
        out_specs=local,
        compiler_params=params,
    )(where, mine, twin, other, other_twin)
    return (weights, new_first, new_second, new_master, new_average)


def solution(mesh):
    shape = dict(zip(mesh.axis_names, mesh.devices.shape))
    nx, ny = 4, shape["dp"] // 8
    fine = Mesh(
        mesh.devices.reshape(nx, ny, 2, shape["tensor"], shape["replica"]),
        ("x", "y", "core", "tensor", "replica"),
    )
    groups = ("x", "y", "core", "replica")
    state = P(None, groups, "tensor")
    placed = (
        P(groups, "tensor", None),
        P(groups, None, None, "tensor"),
        state,
        state,
        state,
        P(groups, "tensor", None, None),
    )
    return jax.shard_map(
        shards,
        mesh=fine,
        in_specs=placed,
        out_specs=(P(None, None, "tensor"), state, state, state, P(groups, "tensor", None, None)),
        check_vma=False,
    )
```
